32 devices in a mesh: groups: 2 (over y), ctx: 4 (over z), head: 2 (over x), feat: 2 (over core).
Axes of the slice: x: 2, y: 2, z: 4, core: 2. Of those that a mesh axis runs over, the one named last changes fastest.
Arguments:
- queries: bfloat16 [1024, 5120], P(('groups', 'ctx'), 'head'), parts along dimension 0, may hold values from -6 to 6
- keys: bfloat16 [1024, 1024], P(('groups', 'ctx'), 'head'), parts along dimension 0, may hold values from -6 to 6
- values: bfloat16 [1024, 1024], P(('groups', 'ctx'), 'head'), parts along dimension 0, may hold values from -6 to 6
- log_gate: float32 [1024, 8], P(('groups', 'ctx'), 'head'), parts along dimension 0, may hold values from -1 to 0, as said below
- cand_q: bfloat16 [128, 5120], P('groups', 'head'), parts along dimension 0, may hold values from -12 to 12
- cand_kv: bfloat16 [128, 2, 1024], P('groups', None, 'head'), parts along dimension 0, may hold values from -12 to 12
- token_ids: int32 [32], P('groups'), parts along dimension 0, may hold values from 0 to 63
- fork_pos: int32 [32], P('groups'), parts along dimension 0, may hold values from 1 to 4
- slot_map: int32 [32], P('groups'), parts along dimension 0, may hold values from 0 to 15, each once
Outputs:
- prefill_out: bfloat16 [1024, 5120], P(('groups', 'ctx', 'feat'), 'head'), parts along dimension 0
- branch_out: bfloat16 [32, 5120], P(('groups', 'ctx', 'feat'), 'head'), parts along dimension 0
The draws below stay inside these ranges and needn't reach their ends.
There are 2 independent parts, one for each index of `groups`. The reference program is written for one: setup_inputs(seed, part) draws one part's arguments, and reference() takes and returns one part's arrays. A program takes and returns all parts, laid end to end along the dimension named above; each array names one. Nothing has to cross between parts.
Inputs may be any that keep to these rules, and one draw needn't show every extreme that they name: log_gate is never positive.
All inputs are finite; a program needn't handle non-finite values.
Results may differ from the reference program's by a relative error of at most 0.0055.
Values may be sent and summed in bfloat16 or wider, within the bound.
No kernel may reach another device: no remote copies, remote signals or barrier semaphores. Data moves between devices by JAX's collectives and lax.ppermute only.
A program may use at most 192 MiB of HBM per device.

```python
import math
import jax
import jax.numpy as jnp
import numpy as np
from jax import lax

HEAD = 128
QHEADS = 40
LOOKUP_GROUPS = 8
TOK_DEV = 128
CANDS = 64
GROUP = 5
FEATS = 8256
CONTEXT_LENGTH = 512
BRANCHES = 16
N_CTX = 4


def draw_log_gate(key, part):
    complete_lookup_vectors = jax.random.split(key, 7)
    blocks = CONTEXT_LENGTH // TOK_DEV
    fast_share = 0.5
    fast = jax.random.uniform(complete_lookup_vectors[0], (LOOKUP_GROUPS,), jnp.float32) < fast_share
    fast_rate = 1.0 / jax.random.uniform(complete_lookup_vectors[1], (LOOKUP_GROUPS,), jnp.float32, 30.0, 50.0)
    slow_rate = jax.random.uniform(complete_lookup_vectors[2], (LOOKUP_GROUPS,), jnp.float32, 0.1, 0.8) / CONTEXT_LENGTH
    base = jnp.where(fast, fast_rate, slow_rate)
    block_factor = jnp.exp(jax.random.uniform(complete_lookup_vectors[3], (blocks, 1, LOOKUP_GROUPS), jnp.float32, -0.7, 0.7))
    jitter = jax.random.uniform(complete_lookup_vectors[4], (blocks, TOK_DEV, LOOKUP_GROUPS), jnp.float32, 0.5, 1.5)
    forgetting_speed = (base[None, None, :] * block_factor * jitter).reshape(CONTEXT_LENGTH, LOOKUP_GROUPS)
    sampled_item_lines = jax.random.randint(complete_lookup_vectors[5], (2, LOOKUP_GROUPS), 0, CONTEXT_LENGTH)
    sequence_places = jnp.arange(CONTEXT_LENGTH)[:, None, None]
    causal_allowance = jnp.any(sequence_places == sampled_item_lines[None, :, :], axis=1)
    decoded_item_group = jnp.log(jax.random.uniform(complete_lookup_vectors[6], (CONTEXT_LENGTH, LOOKUP_GROUPS), jnp.float32, 0.5, 0.8))
    return (-forgetting_speed + jnp.where(causal_allowance, decoded_item_group, 0.0)).astype(jnp.float32)


def touch_ends(values, rng, low, largest):
    place = [jax.random.randint(jax.random.fold_in(rng, axis), (), 0, length) for axis, length in enumerate(values.shape)]
    main_axis = values.shape.index(max(values.shape))
    beside = place[:main_axis] + [(place[main_axis] + 1) % values.shape[main_axis]] + place[main_axis + 1:]
    return values.at[tuple(place)].set(low).at[tuple(beside)].set(largest)


def block_levels(key, dims, cuts, low, high):
    def one(axis_at, shards_of):
        heights = jax.random.uniform(jax.random.fold_in(jax.random.fold_in(key, 6), axis_at), (shards_of,), jnp.float32, low / len(cuts), high / len(cuts))
        return jnp.repeat(jnp.exp(heights), dims[axis_at] // shards_of).reshape((-1,) + (1,) * (len(dims) - axis_at - 1))

    level = one(*cuts[0])
    for cut in cuts[1:]:
        level = level * one(*cut)
    return level


def bell_draw(own_key, dims, scale, reach, cuts=(), kind=jnp.bfloat16):
    result = jax.random.normal(own_key, dims, jnp.float32) * scale
    if len(cuts) > 0:
        result = block_levels(own_key, dims, cuts, -0.22, 0.18) * result
    return jnp.clip(result, min=-reach, max=reach).astype(kind)


def setup_inputs(seed: int = 0, part: int = 0) -> dict:
    seeds = jax.random.split(jax.random.key(seed), 10)
    part_keys = jax.random.split(jax.random.fold_in(seeds[9], part), 10)
    return {
        "queries": bell_draw(part_keys[0], (CONTEXT_LENGTH, QHEADS * HEAD), 1.0, 6.0, ((0, 4), (1, 2))),
        "keys": bell_draw(part_keys[1], (CONTEXT_LENGTH, LOOKUP_GROUPS * HEAD), 1.0, 6.0, ((0, 4), (1, 2))),
        "values": bell_draw(part_keys[2], (CONTEXT_LENGTH, LOOKUP_GROUPS * HEAD), 1.0, 6.0, ((0, 4), (1, 2))),
        "log_gate": draw_log_gate(jax.random.fold_in(jax.random.fold_in(seeds[9], part), 71), part),
        "cand_q": bell_draw(part_keys[4], (CANDS, QHEADS * HEAD), 2.0, 12.0, ((1, 2),)),
        "cand_kv": bell_draw(part_keys[5], (CANDS, 2, LOOKUP_GROUPS * HEAD), 2.0, 12.0, ((2, 2),)),
        "token_ids": touch_ends(jax.random.randint(part_keys[6], (BRANCHES,), 0, CANDS), jax.random.fold_in(part_keys[6], 1), 0, CANDS - 1).astype(jnp.int32),
        "fork_pos": touch_ends(jax.random.randint(part_keys[7], (BRANCHES,), 1, N_CTX + 1), jax.random.fold_in(part_keys[7], 1), 1, N_CTX).astype(jnp.int32),
        "slot_map": jax.random.permutation(part_keys[8], BRANCHES).astype(jnp.int32),
    }


def pair_tables():
    left, right = np.triu_indices(HEAD)
    coef = np.where(left == right, 1.0, math.sqrt(2.0))
    return (jnp.asarray(left, jnp.int32), jnp.asarray(right, jnp.int32), jnp.asarray(coef, jnp.float32))

def expand(block, left, right, coef):
    wide = block.astype(jnp.float32)
    return (jnp.take(wide, left, axis=1) * jnp.take(wide, right, axis=1) * coef).astype(jnp.bfloat16)

def reference(queries, keys, values, log_gate, cand_q, cand_kv, token_ids, fork_pos, slot_map):
    left, right, coef = pair_tables()
    highest = lax.Precision.HIGHEST
    spans = CONTEXT_LENGTH // TOK_DEV
    q_blocks = queries.reshape(spans, TOK_DEV, QHEADS * HEAD)
    k_blocks = keys.reshape(spans, TOK_DEV, LOOKUP_GROUPS * HEAD)
    v_blocks = values.reshape(spans, TOK_DEV, LOOKUP_GROUPS * HEAD)
    g_blocks = log_gate.reshape(spans, TOK_DEV, LOOKUP_GROUPS)
    new_q = cand_q[token_ids]
    new_k = cand_kv[token_ids, 0]
    new_v = cand_kv[token_ids, 1]
    phi_new = [expand(new_q[:, g * HEAD:(g + 1) * HEAD], left, right, coef).astype(jnp.float32) for g in range(QHEADS)]
    rowpos = lax.broadcasted_iota(jnp.int32, (TOK_DEV, TOK_DEV), 0)
    colpos = lax.broadcasted_iota(jnp.int32, (TOK_DEV, TOK_DEV), 1)
    causal = colpos <= rowpos

    def span_step(carry, inputs):
        states, norms, dec_num, dec_den = carry
        q_blk, k_blk, v_blk, g_blk, index = inputs
        cumul = jnp.cumsum(g_blk, axis=0)
        finals = cumul[-1]
        carry_w = jnp.exp(finals[None, :] - cumul)
        chosen = (fork_pos - 1 == index).astype(jnp.float32)
        outs = []
        next_states = []
        next_norms = []
        dnum_list = []
        dden_list = []
        for head in range(LOOKUP_GROUPS):
            key_h = k_blk[:, head * HEAD:(head + 1) * HEAD]
            value_h = v_blk[:, head * HEAD:(head + 1) * HEAD]
            phik = expand(key_h, left, right, coef).astype(jnp.float32)
            scaled = (carry_w[:, head:head + 1] * value_h.astype(jnp.float32)).astype(jnp.bfloat16).astype(jnp.float32)
            local_s = jnp.dot(phik.T, scaled, precision=highest)
            local_z = jnp.dot(carry_w[:, head].astype(jnp.bfloat16).astype(jnp.float32), phik, precision=highest)
            prior_s = states[head].astype(jnp.bfloat16).astype(jnp.float32)
            prior_z = norms[head].astype(jnp.bfloat16).astype(jnp.float32)
            growth = jnp.exp(cumul[:, head])
            spread = cumul[:, head][:, None] - cumul[:, head][None, :]
            fading = jnp.where(causal, jnp.exp(jnp.where(causal, spread, 0.0)), 0.0)
            incl_s = jnp.exp(finals[head]) * states[head] + local_s
            incl_z = jnp.exp(finals[head]) * norms[head] + local_z
            incl_sb = incl_s.astype(jnp.bfloat16).astype(jnp.float32)
            incl_zb = incl_z.astype(jnp.bfloat16).astype(jnp.float32)
            for member in range(GROUP):
                column = (head * GROUP + member) * HEAD
                q_h = q_blk[:, column:column + HEAD]
                phiq = expand(q_h, left, right, coef).astype(jnp.float32)
                inter_num = jnp.dot(phiq, prior_s, precision=highest) * growth[:, None] / HEAD
                inter_den = jnp.dot(phiq, prior_z, precision=highest) * growth / HEAD
                raw = jnp.dot(q_h, key_h.T, preferred_element_type=jnp.float32)
                weights = raw * raw / HEAD * fading
                numer = inter_num + jnp.dot(weights.astype(jnp.bfloat16), value_h, preferred_element_type=jnp.float32)
                denom = inter_den + lax.optimization_barrier(jnp.sum(weights, axis=1))
                outs.append((numer / jnp.maximum(denom, 1.0)[:, None]).astype(jnp.bfloat16))
                phin = phi_new[head * GROUP + member]
                dnum_list.append(jnp.dot(phin, incl_sb, precision=highest) * chosen[:, None] / HEAD)
                dden_list.append(jnp.dot(phin, incl_zb, precision=highest) * chosen / HEAD)
            next_states.append(incl_s)
            next_norms.append(incl_z)
        dec_num = dec_num + jnp.concatenate(dnum_list, axis=1)
        dec_den = dec_den + jnp.stack(dden_list, axis=1)
        return ((jnp.stack(next_states), jnp.stack(next_norms), dec_num, dec_den), jnp.concatenate(outs, axis=1))
    start = (jnp.zeros((LOOKUP_GROUPS, FEATS, HEAD), jnp.float32), jnp.zeros((LOOKUP_GROUPS, FEATS), jnp.float32), jnp.zeros((BRANCHES, QHEADS * HEAD), jnp.float32), jnp.zeros((BRANCHES, QHEADS), jnp.float32))
    indices = jnp.arange(spans).astype(jnp.int32)
    final, prefill = lax.scan(span_step, start, (q_blocks, k_blocks, v_blocks, g_blocks, indices))
    dec_num, dec_den = (final[2], final[3])
    pieces = []
    for head in range(LOOKUP_GROUPS):
        key_n = new_k[:, head * HEAD:(head + 1) * HEAD].astype(jnp.float32)
        value_n = new_v[:, head * HEAD:(head + 1) * HEAD].astype(jnp.float32)
        for member in range(GROUP):
            index = head * GROUP + member
            query_n = new_q[:, index * HEAD:(index + 1) * HEAD].astype(jnp.float32)
            inner = lax.optimization_barrier(jnp.sum(query_n * key_n, axis=1))
            own = inner * inner / HEAD
            numer = dec_num[:, index * HEAD:(index + 1) * HEAD] + own[:, None] * value_n
            denom = dec_den[:, index] + own
            pieces.append((numer / jnp.maximum(denom, 1.0)[:, None]).astype(jnp.bfloat16))
    ordered = jnp.concatenate(pieces, axis=1)
    branch_out = jnp.zeros((BRANCHES, QHEADS * HEAD), jnp.bfloat16).at[slot_map].set(ordered)
    return (prefill.reshape(CONTEXT_LENGTH, QHEADS * HEAD), branch_out)
```

```python
import functools

import jax
import jax.numpy as jnp
from jax import lax
from jax.experimental import pallas as pl
from jax.experimental.pallas import tpu as pltpu
from jax.sharding import PartitionSpec as P

HEAD = 128
GROUP = 5
GATE_ROWS = 16
MASKED = -1e30


def dot(a, b, contract, precision=None):
    return lax.dot_general(
        a, b, ((contract[:1], contract[1:]), ((), ())),
        precision=precision, preferred_element_type=jnp.float32,
    )


def exact_dot(a, b, contract):
    return dot(a, b, contract, lax.Precision.HIGHEST)


def gate_sums(log_gate):
    length = log_gate.shape[0]
    row = lax.broadcasted_iota(jnp.int32, (length, length), 0)
    col = lax.broadcasted_iota(jnp.int32, (length, length), 1)
    after = exact_dot(log_gate, (row > col).astype(jnp.float32), (0, 0))
    upto = exact_dot(log_gate, (row <= col).astype(jnp.float32), (0, 0))
    return after, upto


def split3(x):
    high = x.astype(jnp.bfloat16)
    rest = x - high.astype(jnp.float32)
    middle = rest.astype(jnp.bfloat16)
    low = (rest - middle.astype(jnp.float32)).astype(jnp.bfloat16)
    return [part.astype(jnp.float32) for part in (high, middle, low)]


def pack_kernel(k_ref, v_ref, g_ref, out_ref):
    length, width = k_ref.shape
    first_core = lax.axis_index("feat") == 0

    @pl.when(first_core)
    def _():
        out_ref[:length, :] = k_ref[...]

    @pl.when(jnp.logical_not(first_core))
    def _():
        out_ref[:length, :] = v_ref[...]

    after, upto = gate_sums(g_ref[...])
    place = lax.broadcasted_iota(jnp.int32, (GATE_ROWS, length), 0)
    for head in range(width // HEAD):
        total = jnp.broadcast_to(upto[head : head + 1, length - 1 :], (1, length))
        parts = split3(after[head : head + 1, :]) + split3(total)
        tile = jnp.zeros((GATE_ROWS, length), jnp.float32)
        for i, part in enumerate(parts):
            tile = jnp.where(place == i, part, tile)
        out_ref[length:, head * HEAD : (head + 1) * HEAD] = tile.astype(jnp.bfloat16)


def main_kernel(n_ctx, n_feat, partners, *refs):
    (q_ref, k_ref, v_ref, g_ref, cq_ref, ckv_ref, tok_ref, fork_ref, slot_ref) = refs[:9]
    near = refs[9 : 9 + len(partners)]
    far = refs[9 + len(partners) : 9 + 2 * len(partners)]
    out_ref, branch_ref, w_ref, value_ref, row_ref = refs[9 + 2 * len(partners) :]

    ctx = lax.axis_index("ctx")
    feat = lax.axis_index("feat")
    length, width = k_ref.shape
    heads = width // HEAD
    rows = out_ref.shape[0]
    owned = branch_ref.shape[0]
    padded = w_ref.shape[0] - GROUP * rows
    branches = tok_ref.shape[1]
    first_core = feat == 0
    start = pl.multiple_of(feat * rows, rows)
    blocks = [ctx] + [partner(ctx) for partner in partners]

    gate = g_ref[...]
    after, upto = gate_sums(gate)
    row = lax.broadcasted_iota(jnp.int32, (rows, length), 0) + start
    col = lax.broadcasted_iota(jnp.int32, (rows, length), 1)
    causal = col <= row
    row_sum = exact_dot(causal.astype(jnp.float32), gate, (1, 0))

    line = lax.broadcasted_iota(jnp.int32, (padded, 1), 0)
    slot = (ctx * n_feat + feat) * owned + lax.rem(line, owned)
    mine = slot_ref[...] == slot
    pick_id = jnp.sum(jnp.where(mine, tok_ref[...].astype(jnp.float32), 0.0), axis=1, keepdims=True)
    fork = jnp.sum(jnp.where(mine, fork_ref[...].astype(jnp.float32), 0.0), axis=1, keepdims=True)
    fork = fork.astype(jnp.int32)
    cands = cq_ref.shape[0]
    pick = (
        lax.broadcasted_iota(jnp.int32, (padded, cands), 1).astype(jnp.float32) == pick_id
    ).astype(jnp.bfloat16)

    value_ref[:, HEAD:] = jnp.ones((value_ref.shape[0], HEAD), jnp.bfloat16)
    scale = 1.0 / HEAD
    for head in range(heads):
        lanes = slice(head * HEAD, (head + 1) * HEAD)
        tails, totals, keys = [after[head : head + 1, :]], [], [k_ref[:, lanes]]
        totals.append(jnp.broadcast_to(upto[head : head + 1, length - 1 :], (1, length)))
        value_ref[:length, :HEAD] = v_ref[:, lanes]
        for i in range(len(partners)):
            part = near[i][length:, lanes].astype(jnp.float32)
            tails.append(part[0:1] + part[1:2] + part[2:3])
            totals.append(part[3:4] + part[4:5] + part[5:6])
            here, there = near[i][:length, lanes], far[i][:length, lanes]
            keys.append(jnp.where(first_core, here, there))
            value_ref[(i + 1) * length : (i + 2) * length, :HEAD] = jnp.where(
                first_core, there, here
            )

        picked = dot(pick, cq_ref[:, head * GROUP * HEAD : (head + 1) * GROUP * HEAD], (1, 0))
        branch_q = jnp.zeros((padded, HEAD), jnp.float32)
        for member in range(GROUP):
            chosen = (line >= member * owned) & (line < (member + 1) * owned)
            branch_q = jnp.where(chosen, picked[:, member * HEAD : (member + 1) * HEAD], branch_q)
        q_parts = [
            q_ref[pl.ds(start, rows), (head * GROUP + member) * HEAD : (head * GROUP + member + 1) * HEAD]
            for member in range(GROUP)
        ]
        q_all = jnp.concatenate(q_parts + [branch_q.astype(jnp.bfloat16)], axis=0)
        row_h = row_sum[:, head : head + 1]
        for b, block in enumerate(blocks):
            raw = dot(q_all, keys[b], (1, 1))
            square = raw * raw
            if b == 0:
                reach = jnp.where(causal, row_h - upto[head : head + 1, :], MASKED)
            else:
                between = jnp.zeros((1, length), jnp.float32)
                for o, other in enumerate(blocks):
                    if o not in (0, b):
                        inside = (other > block) & (other < ctx)
                        between = between + jnp.where(inside, totals[o], 0.0)
                reach = jnp.where(block < ctx, row_h + (between + tails[b]), MASKED)
            decay = jnp.exp(reach) * scale
            past = jnp.broadcast_to(tails[b], (padded, length))
            for o, other in enumerate(blocks):
                if o != b:
                    inside = (other > block) & (other < fork)
                    past = past + jnp.where(inside, totals[o], 0.0)
            branch_decay = jnp.exp(jnp.where(block < fork, past, MASKED)) * scale
            cols = slice(b * length, (b + 1) * length)
            for member in range(GROUP):
                span = slice(member * rows, (member + 1) * rows)
                w_ref[span, cols] = (square[span] * decay).astype(jnp.bfloat16)
            w_ref[GROUP * rows :, cols] = (square[GROUP * rows :] * branch_decay).astype(
                jnp.bfloat16
            )
        total = dot(w_ref[...], value_ref[...], (1, 0))
        prefill = total[: GROUP * rows]
        ratio = prefill[:, :HEAD] / jnp.maximum(prefill[:, HEAD:], 1.0)
        for member in range(GROUP):
            column = (head * GROUP + member) * HEAD
            out_ref[:, column : column + HEAD] = ratio[member * rows : (member + 1) * rows].astype(
                out_ref.dtype
            )
        new_k = dot(pick, ckv_ref[:, lanes], (1, 0))
        new_v = dot(pick, ckv_ref[:, width + head * HEAD : width + (head + 1) * HEAD], (1, 0))
        inner = jnp.sum(branch_q * new_k, axis=1, keepdims=True)
        own = inner * inner * scale
        branch = total[GROUP * rows :]
        row_ref[...] = (branch[:, :HEAD] + own * new_v) / jnp.maximum(branch[:, HEAD:] + own, 1.0)
        for member in range(GROUP):
            column = (head * GROUP + member) * HEAD
            branch_ref[:, column : column + HEAD] = row_ref[
                member * owned : (member + 1) * owned, :
            ].astype(branch_ref.dtype)


def swaps(count):
    if count & (count - 1) == 0:
        return [
            ([(i, i ^ step) for i in range(count)], functools.partial(lambda s, i: i ^ s, step))
            for step in range(1, count)
        ]
    return [
        (
            [(i, (i + step) % count) for i in range(count)],
            functools.partial(lambda s, i: lax.rem(i + count - s, count), step),
        )
        for step in range(1, count)
    ]


def per_device(queries, keys, values, log_gate, cand_q, cand_kv, token_ids, fork_pos, slot_map):
    n_ctx = lax.axis_size("ctx")
    n_feat = lax.axis_size("feat")
    length, width = keys.shape
    rows = length // n_feat
    branches = token_ids.shape[0]
    owned = branches // (n_ctx * n_feat)
    padded = -(-GROUP * owned // 16) * 16
    assert n_feat == 2 and length == HEAD

    whole = pl.BlockSpec(memory_space=pltpu.VMEM)
    payload = pl.pallas_call(
        pack_kernel,
        out_shape=jax.ShapeDtypeStruct((length + GATE_ROWS, width), jnp.bfloat16),
        in_specs=[whole] * 3,
        out_specs=whole,
        name="pack",
    )(keys, values, log_gate)
    pairings = swaps(n_ctx)
    order = [1, 0] + list(range(2, len(pairings)))
    near, far = {}, {}
    for step in order:
        near[step] = lax.ppermute(payload, "ctx", pairings[step][0])
    for step in order:
        far[step] = lax.ppermute(near[step], "feat", [(0, 1), (1, 0)])
    steps = range(len(pairings))

    operands = [
        queries, keys, values, log_gate, cand_q, cand_kv.reshape(cand_kv.shape[0], -1),
        token_ids[None], fork_pos[None], slot_map[None],
        *[near[s] for s in steps], *[far[s] for s in steps],
    ]
    return pl.pallas_call(
        functools.partial(main_kernel, n_ctx, n_feat, [pairings[s][1] for s in steps]),
        out_shape=(
            jax.ShapeDtypeStruct((rows, queries.shape[1]), jnp.bfloat16),
            jax.ShapeDtypeStruct((owned, queries.shape[1]), jnp.bfloat16),
        ),
        in_specs=[whole] * len(operands),
        out_specs=(whole, whole),
        scratch_shapes=[
            pltpu.VMEM((GROUP * rows + padded, n_ctx * length), jnp.bfloat16),
            pltpu.VMEM((n_ctx * length, 2 * HEAD), jnp.bfloat16),
            pltpu.VMEM((padded, HEAD), jnp.float32),
        ],
        name="retention",
    )(*operands)


def solution(mesh):
    return jax.shard_map(
        per_device,
        mesh=mesh,
        in_specs=(
            P(("groups", "ctx"), "head"),
            P(("groups", "ctx"), "head"),
            P(("groups", "ctx"), "head"),
            P(("groups", "ctx"), "head"),
            P("groups", "head"),
            P("groups", None, "head"),
            P("groups"),
            P("groups"),
            P("groups"),
        ),
        out_specs=(P(("groups", "ctx", "feat"), "head"), P(("groups", "ctx", "feat"), "head")),
        check_vma=False,
    )
```

```python
import functools

import jax
import jax.numpy as jnp
from jax import lax
from jax.experimental import pallas as pl
from jax.experimental.pallas import tpu as pltpu
from jax.sharding import PartitionSpec as P


HEAD = 128
GROUP = 5
GATE_ROWS = 8
MASKED = -1e30
SCALE = 1.0 / HEAD


def dot(a, b, contract, precision=None):
    return lax.dot_general(
        a, b, ((contract[:1], contract[1:]), ((), ())),
        precision=precision, preferred_element_type=jnp.float32,
    )


def exact_dot(a, b, contract):
    return dot(a, b, contract, lax.Precision.HIGHEST)


def gate_sums(gate):
    length = gate.shape[1]
    row = lax.broadcasted_iota(jnp.int32, (length, length), 0)
    col = lax.broadcasted_iota(jnp.int32, (length, length), 1)
    after = exact_dot(gate, (row > col).astype(jnp.float32), (1, 0))
    upto = exact_dot(gate, (row <= col).astype(jnp.float32), (1, 0))
    return after, upto


def split3(x):
    high = x.astype(jnp.bfloat16)
    rest = x - high.astype(jnp.float32)
    middle = rest.astype(jnp.bfloat16)
    low = (rest - middle.astype(jnp.float32)).astype(jnp.bfloat16)
    return [part.astype(jnp.float32) for part in (high, middle, low)]


def pack_kernel(k_ref, v_ref, g_ref, out_ref, gate_ref, sem):
    length, width = k_ref.shape
    body = out_ref.at[pl.ds(0, length), :]
    from_k = pltpu.make_async_copy(k_ref, body, sem.at[0])
    from_v = pltpu.make_async_copy(v_ref, body, sem.at[0])
    gates = pltpu.make_async_copy(g_ref, gate_ref, sem.at[1])
    first_core = lax.axis_index("feat") == 0
    gates.start()
    pl.when(first_core)(from_k.start)
    pl.when(jnp.logical_not(first_core))(from_v.start)
    gates.wait()
    after, upto = gate_sums(gate_ref[...])
    place = lax.broadcasted_iota(jnp.int32, (GATE_ROWS, length), 0)
    for head in range(width // HEAD):
        total = jnp.broadcast_to(upto[head : head + 1, length - 1 :], (1, length))
        parts = split3(after[head : head + 1, :]) + split3(total)
        tile = jnp.zeros((GATE_ROWS, length), jnp.float32)
        for i, part in enumerate(parts):
            tile = jnp.where(place == i, part, tile)
        out_ref[length:, head * HEAD : (head + 1) * HEAD] = tile.astype(jnp.bfloat16)
    pl.when(first_core)(from_k.wait)
    pl.when(jnp.logical_not(first_core))(from_v.wait)


def own_kernel(n_feat, *refs):
    sources, outs, bufs, sem = refs[:9], refs[9:15], refs[15:24], refs[24]
    queries_acc = outs
    qa_ref, acc_ref, own_ref, row_ref, fork_out, gate_out = queries_acc
    q_ref, k_ref, v_ref, g_ref, cq_ref, ckv_ref, tok_ref, fork_ref, slot_ref = bufs

    ctx = lax.axis_index("ctx")
    feat = lax.axis_index("feat")
    rows = q_ref.shape[0]
    length, width = k_ref.shape
    heads = width // HEAD
    padded = qa_ref.shape[1] - GROUP * rows
    start = pl.multiple_of(feat * rows, rows)
    copies = []
    for i, (source, buf) in enumerate(zip(sources, bufs)):
        origin = source.at[pl.ds(start, rows), :] if i == 0 else source
        copies.append(pltpu.make_async_copy(origin, buf, sem.at[i]))
    for copy in copies:
        copy.start()
    for copy in copies:
        copy.wait()

    gate = g_ref[...]
    after, upto = gate_sums(gate)
    gate_out[:heads, :] = after
    gate_out[heads:, :] = jnp.broadcast_to(upto[:, length - 1 :], (heads, length))
    row = lax.broadcasted_iota(jnp.int32, (rows, length), 0) + start
    col = lax.broadcasted_iota(jnp.int32, (rows, length), 1)
    causal = col <= row
    row_sum = exact_dot(causal.astype(jnp.float32), gate, (1, 1))
    row_ref[...] = row_sum

    owned = tok_ref.shape[1] // (lax.axis_size("ctx") * n_feat)
    line = lax.broadcasted_iota(jnp.int32, (padded, 1), 0)
    slot = (ctx * n_feat + feat) * owned + lax.rem(line, owned)
    mine = slot_ref[...] == slot
    pick_id = jnp.sum(jnp.where(mine, tok_ref[...].astype(jnp.float32), 0.0), axis=1, keepdims=True)
    fork = jnp.sum(jnp.where(mine, fork_ref[...].astype(jnp.float32), 0.0), axis=1, keepdims=True)
    fork_out[...] = jnp.broadcast_to(fork.astype(jnp.int32), fork_out.shape)
    cands = cq_ref.shape[0]
    pick = (
        lax.broadcasted_iota(jnp.int32, (padded, cands), 1).astype(jnp.float32) == pick_id
    ).astype(jnp.bfloat16)

    ones = jnp.ones((length, HEAD), jnp.bfloat16)
    for head in range(heads):
        lanes = slice(head * HEAD, (head + 1) * HEAD)
        picked = dot(pick, cq_ref[:, head * GROUP * HEAD : (head + 1) * GROUP * HEAD], (1, 0))
        branch_q = jnp.zeros((padded, HEAD), jnp.float32)
        for member in range(GROUP):
            chosen = (line >= member * owned) & (line < (member + 1) * owned)
            branch_q = jnp.where(chosen, picked[:, member * HEAD : (member + 1) * HEAD], branch_q)
        for member in range(GROUP):
            column = (head * GROUP + member) * HEAD
            qa_ref[head, member * rows : (member + 1) * rows, :] = q_ref[:, column : column + HEAD]
        qa_ref[head, GROUP * rows :, :] = branch_q.astype(jnp.bfloat16)

        reach = jnp.where(causal, row_sum[:, head : head + 1] - upto[head : head + 1, :], MASKED)
        decay = jnp.exp(reach) * SCALE
        branch_decay = jnp.exp(after[head : head + 1, :]) * SCALE
        raw = dot(qa_ref[head], k_ref[:, lanes], (1, 1))
        square = raw * raw
        weights = [
            (square[m * rows : (m + 1) * rows] * decay).astype(jnp.bfloat16) for m in range(GROUP)
        ]
        weights.append((square[GROUP * rows :] * branch_decay).astype(jnp.bfloat16))
        value = jnp.concatenate([v_ref[:, lanes], ones], axis=1)
        acc_ref[head] = dot(jnp.concatenate(weights, axis=0), value, (1, 0))

        new_k = dot(pick, ckv_ref[:, 0, lanes], (1, 0))
        new_v = dot(pick, ckv_ref[:, 1, lanes], (1, 0))
        inner = jnp.sum(branch_q * new_k, axis=1, keepdims=True)
        weight = inner * inner * SCALE
        own_ref[head, :, :HEAD] = weight * new_v
        own_ref[head, :, HEAD:] = jnp.broadcast_to(weight, (padded, HEAD))


def rest_kernel(partners, *refs):
    count = len(partners)
    qa_ref, acc_ref, own_ref, row_ref, fork_ref, gate_ref = refs[:6]
    near, far = refs[6 : 6 + count], refs[6 + count : 6 + 2 * count]
    out_ref, branch_ref, w_ref, value_ref, key_ref, line_ref = refs[6 + 2 * count :]

    ctx = lax.axis_index("ctx")
    first_core = lax.axis_index("feat") == 0
    rows = out_ref.shape[0]
    owned = branch_ref.shape[0]
    heads, total_rows, _ = qa_ref.shape
    padded = total_rows - GROUP * rows
    length = gate_ref.shape[1]
    others = [partner(ctx) for partner in partners]
    fork = fork_ref[...]
    value_ref[:, HEAD:] = jnp.ones((value_ref.shape[0], HEAD), jnp.bfloat16)
    for head in range(heads):
        lanes = slice(head * HEAD, (head + 1) * HEAD)
        row_h = row_ref[:, head : head + 1]
        tails, totals = [], []
        for i in range(count):
            part = near[i][length:, lanes].astype(jnp.float32)
            tails.append(part[0:1] + part[1:2] + part[2:3])
            totals.append(part[3:4] + part[4:5] + part[5:6])
            here, there = near[i][:length, lanes], far[i][:length, lanes]
            key_ref[i * length : (i + 1) * length, :] = jnp.where(first_core, here, there)
            value_ref[i * length : (i + 1) * length, :HEAD] = jnp.where(first_core, there, here)
        raw = dot(qa_ref[head], key_ref[...], (1, 1))
        square = raw * raw
        between_own = jnp.zeros((padded, length), jnp.float32)
        for b, block in enumerate(others):
            between_own = between_own + jnp.where((block > ctx) & (block < fork), totals[b], 0.0)
            between = tails[b]
            past = tails[b] + jnp.where(
                (ctx > block) & (ctx < fork), gate_ref[heads + head : heads + head + 1, :], 0.0
            )
            for o, other in enumerate(others):
                if o != b:
                    between = between + jnp.where((other > block) & (other < ctx), totals[o], 0.0)
                    past = past + jnp.where((other > block) & (other < fork), totals[o], 0.0)
            decay = jnp.exp(jnp.where(block < ctx, row_h + between, MASKED)) * SCALE
            branch_decay = jnp.exp(jnp.where(block < fork, past, MASKED)) * SCALE
            cols = slice(b * length, (b + 1) * length)
            for member in range(GROUP):
                span = slice(member * rows, (member + 1) * rows)
                w_ref[span, cols] = (square[span, cols] * decay).astype(jnp.bfloat16)
            w_ref[GROUP * rows :, cols] = (square[GROUP * rows :, cols] * branch_decay).astype(
                jnp.bfloat16
            )
        total = dot(w_ref[...], value_ref[...], (1, 0))
        prefill = total[: GROUP * rows] + acc_ref[head, : GROUP * rows, :]
        ratio = prefill[:, :HEAD] / jnp.maximum(prefill[:, HEAD:], 1.0)
        for member in range(GROUP):
            column = (head * GROUP + member) * HEAD
            out_ref[:, column : column + HEAD] = ratio[member * rows : (member + 1) * rows].astype(
                out_ref.dtype
            )
        kept = jnp.exp(jnp.where(ctx < fork, between_own, MASKED))
        branch = total[GROUP * rows :] + own_ref[head]
        before = acc_ref[head, GROUP * rows :, :]
        numer = branch[:, :HEAD] + kept * before[:, :HEAD]
        denom = branch[:, HEAD:] + kept * before[:, HEAD:]
        line_ref[...] = numer / jnp.maximum(denom, 1.0)
        for member in range(GROUP):
            column = (head * GROUP + member) * HEAD
            branch_ref[:, column : column + HEAD] = line_ref[
                member * owned : (member + 1) * owned, :
            ].astype(branch_ref.dtype)


def swaps(count):
    if count & (count - 1) == 0:
        return [
            ([(i, i ^ step) for i in range(count)], functools.partial(lambda s, i: i ^ s, step))
            for step in range(1, count)
        ]
    return [
        (
            [(i, (i + step) % count) for i in range(count)],
            functools.partial(lambda s, i: lax.rem(i + count - s, count), step),
        )
        for step in range(1, count)
    ]


ORDER = (2, 1, 3)


def per_device(queries, keys, values, log_gate, cand_q, cand_kv, token_ids, fork_pos, slot_map):
    n_ctx = lax.axis_size("ctx")
    n_feat = lax.axis_size("feat")
    length, width = keys.shape
    heads = width // HEAD
    rows = length // n_feat
    branches = token_ids.shape[0]
    owned = branches // (n_ctx * n_feat)
    padded = -(-GROUP * owned // 16) * 16
    total_rows = GROUP * rows + padded
    assert n_feat == 2 and length == HEAD

    hbm = pl.BlockSpec(memory_space=pltpu.HBM)
    vmem = pl.BlockSpec(memory_space=pltpu.VMEM)
    in_hbm = lambda x: pltpu.with_memory_space_constraint(x, pltpu.HBM)
    gates = in_hbm(log_gate.T)
    payload = pl.pallas_call(
        pack_kernel,
        out_shape=jax.ShapeDtypeStruct((length + GATE_ROWS, width), jnp.bfloat16),
        in_specs=[hbm] * 3,
        out_specs=vmem,
        scratch_shapes=[
            pltpu.VMEM(gates.shape, gates.dtype),
            pltpu.SemaphoreType.DMA((2,)),
        ],
        compiler_params=pltpu.CompilerParams(vmem_limit_bytes=4 << 20),
        name="pack",
    )(in_hbm(keys), in_hbm(values), gates)
    pairings = swaps(n_ctx)
    count = len(pairings)
    steps = [s - 1 for s in ORDER] if count == 3 else list(range(count))
    near, far = [], []
    for s in steps:
        near.append(lax.ppermute(payload, "ctx", pairings[s][0]))
    for part in near:
        far.append(lax.ppermute(part, "feat", [(0, 1), (1, 0)]))
    partners = [pairings[s][1] for s in steps]

    sources = [
        queries, keys, values, gates, cand_q, cand_kv,
        token_ids[None], fork_pos[None], slot_map[None],
    ]
    own = pl.pallas_call(
        functools.partial(own_kernel, n_feat),
        out_shape=(
            jax.ShapeDtypeStruct((heads, total_rows, HEAD), jnp.bfloat16),
            jax.ShapeDtypeStruct((heads, total_rows, 2 * HEAD), jnp.float32),
            jax.ShapeDtypeStruct((heads, padded, 2 * HEAD), jnp.float32),
            jax.ShapeDtypeStruct((rows, heads), jnp.float32),
            jax.ShapeDtypeStruct((padded, length), jnp.int32),
            jax.ShapeDtypeStruct((2 * heads, length), jnp.float32),
        ),
        in_specs=[hbm] * len(sources),
        out_specs=(vmem,) * 6,
        scratch_shapes=[pltpu.VMEM((rows, queries.shape[1]), queries.dtype)]
        + [pltpu.VMEM(s.shape, s.dtype) for s in sources[1:]]
        + [pltpu.SemaphoreType.DMA((len(sources),))],
        compiler_params=pltpu.CompilerParams(vmem_limit_bytes=16 << 20),
        cost_estimate=pl.CostEstimate(flops=1 << 30, bytes_accessed=8 << 20, transcendentals=0),
        name="own",
    )(*[in_hbm(s) for s in sources])
    operands = [*own, *near, *far]
    return pl.pallas_call(
        functools.partial(rest_kernel, partners),
        out_shape=(
            jax.ShapeDtypeStruct((rows, queries.shape[1]), jnp.bfloat16),
            jax.ShapeDtypeStruct((owned, queries.shape[1]), jnp.bfloat16),
        ),
        in_specs=[vmem] * len(operands),
        out_specs=(vmem, vmem),
        scratch_shapes=[
            pltpu.VMEM((total_rows, count * length), jnp.bfloat16),
            pltpu.VMEM((count * length, 2 * HEAD), jnp.bfloat16),
            pltpu.VMEM((count * length, HEAD), jnp.bfloat16),
            pltpu.VMEM((padded, HEAD), jnp.float32),
        ],
        compiler_params=pltpu.CompilerParams(vmem_limit_bytes=16 << 20),
        name="rest",
    )(*operands)


def solution(mesh):
    return sharded(mesh)


def sharded(mesh):
    return jax.shard_map(
        per_device,
        mesh=mesh,
        in_specs=(
            P(("groups", "ctx"), "head"),
            P(("groups", "ctx"), "head"),
            P(("groups", "ctx"), "head"),
            P(("groups", "ctx"), "head"),
            P("groups", "head"),
            P("groups", None, "head"),
            P("groups"),
            P("groups"),
            P("groups"),
        ),
        out_specs=(P(("groups", "ctx", "feat"), "head"), P(("groups", "ctx", "feat"), "head")),
        check_vma=False,
    )
```

```python
import functools

import jax
import jax.numpy as jnp
from jax import lax
from jax.experimental import pallas as pl
from jax.experimental.pallas import tpu as pltpu
from jax.sharding import PartitionSpec as P


HEAD = 128
GROUP = 5
MASKED = -1e30
SCALE = 1.0 / HEAD


def dot(a, b, contract, precision=None):
    return lax.dot_general(
        a, b, ((contract[:1], contract[1:]), ((), ())),
        precision=precision, preferred_element_type=jnp.float32,
    )


def exact_dot(a, b, contract):
    return dot(a, b, contract, lax.Precision.HIGHEST)


def triangle(length, keep):
    row = lax.broadcasted_iota(jnp.int32, (length, length), 0)
    col = lax.broadcasted_iota(jnp.int32, (length, length), 1)
    return keep(row, col).astype(jnp.float32)


def from_inclusive(inclusive):
    lane = lax.broadcasted_iota(jnp.int32, inclusive.shape, 1)
    last = inclusive.shape[1] - 1
    after = jnp.where(lane == last, 0.0, pltpu.roll(inclusive, last, 1))
    total = jnp.broadcast_to(inclusive[:, :1], inclusive.shape)
    return after, total


def received_gates(ref, heads, first_core):
    tile = ref[ref.shape[0] - gate_rows(heads) :, :].astype(jnp.float32)
    mixed = tile + pltpu.roll(tile, tile.shape[0] - heads, 0)
    after, total = from_inclusive(mixed)
    after = jnp.where(first_core, after, pltpu.roll(after, after.shape[1] // 2, 1))
    return after, total


def gate_rows(heads):
    return -(-2 * heads // 8) * 8


def pack_kernel(k_ref, v_ref, g_ref, out_ref, gate_ref, sem):
    length, width = k_ref.shape
    heads = width // HEAD
    half = length // 2
    start = pl.multiple_of(lax.axis_index("feat") * half, half)
    gates = pltpu.make_async_copy(g_ref, gate_ref, sem.at[0])
    gates.start()
    copies = []
    for i, ref in enumerate((k_ref, v_ref)):
        for head in range(heads):
            copies.append(
                pltpu.make_async_copy(
                    ref.at[pl.ds(start, half), pl.ds(head * HEAD, HEAD)],
                    out_ref.at[pl.ds((i * heads + head) * half, half), :],
                    sem.at[1 + i * heads + head],
                )
            )
    for copy in copies:
        copy.start()
    gates.wait()
    inclusive = exact_dot(gate_ref[...], triangle(length, lambda r, c: r >= c), (1, 0))
    high = inclusive.astype(jnp.bfloat16).astype(jnp.float32)
    parts = [high, inclusive - high]
    spare = gate_rows(heads) - 2 * heads
    if spare:
        parts.append(jnp.zeros((spare, length), jnp.float32))
    out_ref[2 * heads * half :, :] = jnp.concatenate(parts, axis=0).astype(jnp.bfloat16)
    for copy in copies:
        copy.wait()


def own_kernel(n_feat, *refs):
    sources, outs, bufs, sem = refs[:9], refs[9:15], refs[15:24], refs[24]
    qa_ref, acc_ref, own_ref, row_ref, fork_out, gate_out = outs
    q_ref, k_ref, v_ref, g_ref, cq_ref, ckv_ref, tok_ref, fork_ref, slot_ref = bufs

    ctx = lax.axis_index("ctx")
    feat = lax.axis_index("feat")
    rows = q_ref.shape[0]
    length, width = k_ref.shape
    heads = width // HEAD
    padded = qa_ref.shape[1] - GROUP * rows
    start = pl.multiple_of(feat * rows, rows)
    copies = []
    for i, (source, buf) in enumerate(zip(sources, bufs)):
        origin = source.at[pl.ds(start, rows), :] if i == 0 else source
        copies.append(pltpu.make_async_copy(origin, buf, sem.at[i]))
    for copy in copies:
        copy.start()
    for copy in copies:
        copy.wait()

    gate = g_ref[...]
    upto = exact_dot(gate, triangle(length, lambda r, c: r <= c), (1, 0))
    after = exact_dot(gate, triangle(length, lambda r, c: r > c), (1, 0))
    gate_out[...] = jnp.broadcast_to(upto[:, length - 1 :], (heads, length))
    row = lax.broadcasted_iota(jnp.int32, (rows, length), 0) + start
    col = lax.broadcasted_iota(jnp.int32, (rows, length), 1)
    causal = col <= row
    row_sum = exact_dot(causal.astype(jnp.float32), gate, (1, 1))
    row_ref[...] = row_sum

    owned = tok_ref.shape[1] // (lax.axis_size("ctx") * n_feat)
    line = lax.broadcasted_iota(jnp.int32, (padded, 1), 0)
    slot = (ctx * n_feat + feat) * owned + lax.rem(line, owned)
    mine = slot_ref[...] == slot
    pick_id = jnp.sum(jnp.where(mine, tok_ref[...].astype(jnp.float32), 0.0), axis=1, keepdims=True)
    fork = jnp.sum(jnp.where(mine, fork_ref[...].astype(jnp.float32), 0.0), axis=1, keepdims=True)
    fork_out[...] = jnp.broadcast_to(fork.astype(jnp.int32), fork_out.shape)
    cands = cq_ref.shape[0]
    pick = (
        lax.broadcasted_iota(jnp.int32, (padded, cands), 1).astype(jnp.float32) == pick_id
    ).astype(jnp.bfloat16)

    ones = jnp.ones((length, HEAD), jnp.bfloat16)
    for head in range(heads):
        lanes = slice(head * HEAD, (head + 1) * HEAD)
        picked = dot(pick, cq_ref[:, head * GROUP * HEAD : (head + 1) * GROUP * HEAD], (1, 0))
        branch_q = jnp.zeros((padded, HEAD), jnp.float32)
        for member in range(GROUP):
            chosen = (line >= member * owned) & (line < (member + 1) * owned)
            branch_q = jnp.where(chosen, picked[:, member * HEAD : (member + 1) * HEAD], branch_q)
        for member in range(GROUP):
            column = (head * GROUP + member) * HEAD
            qa_ref[head, member * rows : (member + 1) * rows, :] = q_ref[:, column : column + HEAD]
        qa_ref[head, GROUP * rows :, :] = branch_q.astype(jnp.bfloat16)

        reach = jnp.where(causal, row_sum[:, head : head + 1] - upto[head : head + 1, :], MASKED)
        decay = jnp.exp(reach) * SCALE
        branch_decay = jnp.exp(after[head : head + 1, :]) * SCALE
        raw = dot(qa_ref[head], k_ref[:, lanes], (1, 1))
        square = raw * raw
        weights = [
            (square[m * rows : (m + 1) * rows] * decay).astype(jnp.bfloat16) for m in range(GROUP)
        ]
        weights.append((square[GROUP * rows :] * branch_decay).astype(jnp.bfloat16))
        value = jnp.concatenate([v_ref[:, lanes], ones], axis=1)
        acc_ref[head] = dot(jnp.concatenate(weights, axis=0), value, (1, 0))

        new_k = dot(pick, ckv_ref[:, 0, lanes], (1, 0))
        new_v = dot(pick, ckv_ref[:, 1, lanes], (1, 0))
        inner = jnp.sum(branch_q * new_k, axis=1, keepdims=True)
        weight = inner * inner * SCALE
        own_ref[head, :, :HEAD] = weight * new_v
        own_ref[head, :, HEAD:] = jnp.broadcast_to(weight, (padded, HEAD))


def early_kernel(partners, late_partner, *refs):
    count = len(partners)
    qa_ref, acc_ref, own_ref, row_ref, fork_ref, gate_ref = refs[:6]
    near, far = refs[6 : 6 + count], refs[6 + count : 6 + 2 * count]
    (plain_ref, scaled_ref, late_row_ref, late_branch_ref, wp_ref, ws_ref, value_ref, key_ref) = refs[
        6 + 2 * count :
    ]
    ctx = lax.axis_index("ctx")
    first_core = lax.axis_index("feat") == 0
    rows = row_ref.shape[0]
    heads, total_rows, _ = qa_ref.shape
    padded = total_rows - GROUP * rows
    length = gate_ref.shape[1]
    half = length // 2
    blocks = [partner(ctx) for partner in partners]
    late = late_partner(ctx)
    fork = fork_ref[...]
    value_ref[:, HEAD:] = jnp.ones((value_ref.shape[0], HEAD), jnp.bfloat16)
    gates = [received_gates(ref, heads, first_core) for ref in near]
    zero = jnp.zeros((padded, length), jnp.float32)
    for head in range(heads):
        at = slice(head, head + 1)
        row_h = row_ref[:, at]
        own_total = gate_ref[at, :]
        for i in range(count):
            for j, ref in enumerate((near[i], far[i])):
                here = slice(i * length + j * half, i * length + (j + 1) * half)
                key_ref[here, :] = ref[head * half : (head + 1) * half, :]
                value_ref[here, :HEAD] = ref[(heads + head) * half : (heads + head + 1) * half, :]
        raw = dot(qa_ref[head], key_ref[...], (1, 1))
        square = raw * raw
        kept = zero
        late_row = jnp.zeros((1, length), jnp.float32)
        late_branch = jnp.where((ctx > late) & (ctx < fork), own_total, zero)
        for b, block in enumerate(blocks):
            after, total = gates[b][0][at, :], gates[b][1][at, :]
            kept = kept + jnp.where((block > ctx) & (block < fork), total, 0.0)
            late_row = late_row + jnp.where((block > late) & (block < ctx), total, 0.0)
            late_branch = late_branch + jnp.where((block > late) & (block < fork), total, 0.0)
            between = after
            past = after + jnp.where((ctx > block) & (ctx < fork), own_total, zero)
            for o, other in enumerate(blocks):
                if o != b:
                    step = gates[o][1][at, :]
                    between = between + jnp.where((other > block) & (other < ctx), step, 0.0)
                    past = past + jnp.where((other > block) & (other < fork), step, 0.0)
            decay = jnp.exp(jnp.where(block < ctx, row_h + between, MASKED)) * SCALE
            branch_decay = jnp.exp(jnp.where(block < fork, past, MASKED)) * SCALE
            crossed = (late > block) & (late < ctx)
            branch_crossed = (late > block) & (late < fork)
            cols = slice(b * length, (b + 1) * length)
            for ref, row_part, branch_part in (
                (wp_ref, jnp.where(crossed, 0.0, decay), jnp.where(branch_crossed, 0.0, branch_decay)),
                (ws_ref, jnp.where(crossed, decay, 0.0), jnp.where(branch_crossed, branch_decay, 0.0)),
            ):
                for member in range(GROUP):
                    span = slice(member * rows, (member + 1) * rows)
                    ref[span, cols] = (square[span, cols] * row_part).astype(jnp.bfloat16)
                ref[GROUP * rows :, cols] = (square[GROUP * rows :, cols] * branch_part).astype(
                    jnp.bfloat16
                )
        plain = dot(wp_ref[...], value_ref[...], (1, 0))
        scaled = dot(ws_ref[...], value_ref[...], (1, 0))
        split = GROUP * rows
        plain_ref[head, :split] = plain[:split] + acc_ref[head, :split, :]
        scaled_ref[head, :split] = scaled[:split]
        keep = jnp.exp(jnp.where(ctx < fork, kept, MASKED))
        crossed = (late > ctx) & (late < fork)
        before = acc_ref[head, split:, :]
        for side in range(2):
            part = slice(side * HEAD, (side + 1) * HEAD)
            moved = keep * before[:, part]
            plain_ref[head, split:, part] = (
                plain[split:, part] + own_ref[head, :, part] + jnp.where(crossed, 0.0, moved)
            )
            scaled_ref[head, split:, part] = scaled[split:, part] + jnp.where(crossed, moved, 0.0)
        late_row_ref[at, :] = jnp.where(late < ctx, late_row, MASKED)
        late_branch_ref[head] = jnp.where(late < fork, late_branch, MASKED)


def half_product(qa, ref, head, heads, rows, row_part, branch_part):
    half = row_part.shape[1]
    raw = dot(qa, ref[head * half : (head + 1) * half, :], (1, 1))
    square = raw * raw
    weights = [
        (square[m * rows : (m + 1) * rows] * row_part).astype(jnp.bfloat16) for m in range(GROUP)
    ]
    weights.append((square[GROUP * rows :] * branch_part).astype(jnp.bfloat16))
    value = ref[(heads + head) * half : (heads + head + 1) * half, :]
    value = jnp.concatenate([value, jnp.ones((half, HEAD), jnp.bfloat16)], axis=1)
    return dot(jnp.concatenate(weights, axis=0), value, (1, 0))


def near_kernel(
    qa_ref, row_ref, plain_ref, scaled_ref, late_row_ref, late_branch_ref, near_ref,
    sum_ref, decay_ref, branch_decay_ref,
):
    heads = qa_ref.shape[0]
    rows = row_ref.shape[0]
    half = decay_ref.shape[2]
    first_core = lax.axis_index("feat") == 0
    after, total = received_gates(near_ref, heads, first_core)
    factor = jnp.exp(total)
    for head in range(heads):
        at = slice(head, head + 1)
        decay = jnp.exp(row_ref[:, at] + (late_row_ref[at, :] + after[at, :])) * SCALE
        branch_decay = jnp.exp(late_branch_ref[head] + after[at, :]) * SCALE
        decay_ref[head] = decay[:, half:]
        branch_decay_ref[head] = branch_decay[:, half:]
        part = half_product(
            qa_ref[head], near_ref, head, heads, rows, decay[:, :half], branch_decay[:, :half]
        )
        for side in range(2):
            cols = slice(side * HEAD, (side + 1) * HEAD)
            sum_ref[head, :, cols] = part[:, cols] + (
                plain_ref[head, :, cols] + factor[at, :] * scaled_ref[head, :, cols]
            )


def final_kernel(
    qa_ref, sum_ref, decay_ref, branch_decay_ref, far_ref, out_ref, branch_ref,
    stage_ref, branch_stage_ref, line_ref, sem,
):
    heads = qa_ref.shape[0]
    rows = out_ref.shape[0]
    owned = branch_ref.shape[0]
    split = GROUP * rows
    copies = []
    for head in range(heads):
        total = sum_ref[head] + half_product(
            qa_ref[head], far_ref, head, heads, rows, decay_ref[head], branch_decay_ref[head]
        )
        ratio = total[:, :HEAD] / jnp.maximum(total[:, HEAD:], 1.0)
        line_ref[...] = ratio[split:]
        for member in range(GROUP):
            column = (head * GROUP + member) * HEAD
            lanes = slice(column, column + HEAD)
            stage_ref[:, lanes] = ratio[member * rows : (member + 1) * rows].astype(out_ref.dtype)
            branch_stage_ref[:, lanes] = line_ref[
                member * owned : (member + 1) * owned, :
            ].astype(branch_ref.dtype)
        wide = pl.ds(head * GROUP * HEAD, GROUP * HEAD)
        copies.append(
            pltpu.make_async_copy(stage_ref.at[:, wide], out_ref.at[:, wide], sem.at[head])
        )
        copies[-1].start()
    copies.append(pltpu.make_async_copy(branch_stage_ref, branch_ref, sem.at[heads]))
    copies[-1].start()
    for copy in copies:
        copy.wait()


def swaps(count):
    if count & (count - 1) == 0:
        return [
            ([(i, i ^ step) for i in range(count)], functools.partial(lambda s, i: i ^ s, step))
            for step in range(1, count)
        ]
    return [
        (
            [(i, (i + step) % count) for i in range(count)],
            functools.partial(lambda s, i: lax.rem(i + count - s, count), step),
        )
        for step in range(1, count)
    ]


ORDER = (2, 1, 3)


def call(kernel, operands, outs, scratch=(), vmem=16 << 20, results=None, inputs=None):
    spec = pl.BlockSpec(memory_space=pltpu.VMEM)
    return pl.pallas_call(
        kernel,
        out_shape=outs,
        in_specs=inputs or [spec] * len(operands),
        out_specs=results or (spec,) * len(outs),
        scratch_shapes=list(scratch),
        compiler_params=pltpu.CompilerParams(vmem_limit_bytes=vmem),
        cost_estimate=pl.CostEstimate(flops=1 << 29, bytes_accessed=4 << 20, transcendentals=0),
    )(*operands)


def per_device(queries, keys, values, log_gate, cand_q, cand_kv, token_ids, fork_pos, slot_map):
    n_ctx = lax.axis_size("ctx")
    n_feat = lax.axis_size("feat")
    length, width = keys.shape
    heads = width // HEAD
    rows = length // n_feat
    half = length // 2
    branches = token_ids.shape[0]
    owned = branches // (n_ctx * n_feat)
    padded = -(-GROUP * owned // 16) * 16
    total_rows = GROUP * rows + padded
    assert n_feat == 2 and length == HEAD
    f32, bf16 = jnp.float32, jnp.bfloat16
    shape = jax.ShapeDtypeStruct

    hbm = pl.BlockSpec(memory_space=pltpu.HBM)
    in_hbm = lambda x: pltpu.with_memory_space_constraint(x, pltpu.HBM)
    gates = in_hbm(log_gate.T)
    (payload,) = call(
        pack_kernel, [in_hbm(keys), in_hbm(values), gates],
        (shape((2 * heads * half + gate_rows(heads), HEAD), bf16),),
        [pltpu.VMEM(gates.shape, f32), pltpu.SemaphoreType.DMA((1 + 2 * heads,))],
        vmem=4 << 20, inputs=[hbm] * 3,
    )
    pairings = swaps(n_ctx)
    count = len(pairings)
    steps = [s - 1 for s in ORDER] if count == 3 else list(range(count))
    near, far = [], []
    for s in steps:
        near.append(lax.ppermute(payload, "ctx", pairings[s][0]))
    for part in near:
        far.append(lax.ppermute(part, "feat", [(0, 1), (1, 0)]))
    partners = [pairings[s][1] for s in steps]

    sources = [
        queries, keys, values, gates, cand_q, cand_kv,
        token_ids[None], fork_pos[None], slot_map[None],
    ]
    wide = shape((heads, total_rows, 2 * HEAD), f32)
    queries_all, acc, token, row_sum, fork, total = call(
        functools.partial(own_kernel, n_feat), [in_hbm(s) for s in sources],
        (
            shape((heads, total_rows, HEAD), bf16),
            wide,
            shape((heads, padded, 2 * HEAD), f32),
            shape((rows, heads), f32),
            shape((padded, length), jnp.int32),
            shape((heads, length), f32),
        ),
        [pltpu.VMEM((rows, queries.shape[1]), queries.dtype)]
        + [pltpu.VMEM(s.shape, s.dtype) for s in sources[1:]]
        + [pltpu.SemaphoreType.DMA((len(sources),))],
        inputs=[hbm] * len(sources),
    )
    early = (count - 1) * length
    plain, scaled, late_row, late_branch = call(
        functools.partial(early_kernel, partners[:-1], partners[-1]),
        [queries_all, acc, token, row_sum, fork, total, *near[:-1], *far[:-1]],
        (wide, wide, shape((heads, length), f32), shape((heads, padded, length), f32)),
        [
            pltpu.VMEM((total_rows, early), bf16),
            pltpu.VMEM((total_rows, early), bf16),
            pltpu.VMEM((early, 2 * HEAD), bf16),
            pltpu.VMEM((early, HEAD), bf16),
        ],
    )
    sums, decay, branch_decay = call(
        near_kernel,
        [queries_all, row_sum, plain, scaled, late_row, late_branch, near[-1]],
        (wide, shape((heads, rows, half), f32), shape((heads, padded, half), f32)),
    )
    return call(
        final_kernel, [queries_all, sums, decay, branch_decay, far[-1]],
        (shape((rows, queries.shape[1]), bf16), shape((owned, queries.shape[1]), bf16)),
        [
            pltpu.VMEM((rows, queries.shape[1]), bf16),
            pltpu.VMEM((owned, queries.shape[1]), bf16),
            pltpu.VMEM((padded, HEAD), f32),
            pltpu.SemaphoreType.DMA((heads + 1,)),
        ],
        results=(hbm, hbm),
    )


def solution(mesh):
    return sharded(mesh)


def sharded(mesh):
    return jax.shard_map(
        per_device,
        mesh=mesh,
        in_specs=(
            P(("groups", "ctx"), "head"),
            P(("groups", "ctx"), "head"),
            P(("groups", "ctx"), "head"),
            P(("groups", "ctx"), "head"),
            P("groups", "head"),
            P("groups", None, "head"),
            P("groups"),
            P("groups"),
            P("groups"),
        ),
        out_specs=(P(("groups", "ctx", "feat"), "head"), P(("groups", "ctx", "feat"), "head")),
        check_vma=False,
    )
```

```python
import functools

import jax
import jax.numpy as jnp
from jax import lax
from jax.experimental import pallas as pl
from jax.experimental.pallas import tpu as pltpu
from jax.sharding import PartitionSpec as P


HEAD = 128
GROUP = 5
MASKED = -1e30
SCALE = 1.0 / HEAD


def dot(a, b, contract, precision=None):
    return lax.dot_general(
        a, b, ((contract[:1], contract[1:]), ((), ())),
        precision=precision, preferred_element_type=jnp.float32,
    )


def exact_dot(a, b, contract):
    return dot(a, b, contract, lax.Precision.HIGHEST)


def triangle(length, keep):
    row = lax.broadcasted_iota(jnp.int32, (length, length), 0)
    col = lax.broadcasted_iota(jnp.int32, (length, length), 1)
    return keep(row, col).astype(jnp.float32)


def received_gates(ref, heads, first_core):
    tile = ref[ref.shape[0] - gate_rows(heads) :, :].astype(jnp.float32)
    gate = tile + pltpu.roll(tile, tile.shape[0] - heads, 0)
    length = gate.shape[1]
    after = exact_dot(gate, triangle(length, lambda r, c: r > c), (1, 0))
    total = exact_dot(gate, triangle(length, lambda r, c: r >= 0), (1, 0))
    after = jnp.where(first_core, after, pltpu.roll(after, length // 2, 1))
    return after, total


def gate_rows(heads):
    return -(-2 * heads // 8) * 8


def pack_kernel(k_ref, v_ref, g_ref, out_ref, gate_ref, sem):
    length, width = k_ref.shape
    heads = width // HEAD
    half = length // 2
    start = pl.multiple_of(lax.axis_index("feat") * half, half)
    gates = pltpu.make_async_copy(g_ref, gate_ref, sem.at[0])
    gates.start()
    copies = []
    for i, ref in enumerate((k_ref, v_ref)):
        for head in range(heads):
            copies.append(
                pltpu.make_async_copy(
                    ref.at[pl.ds(start, half), pl.ds(head * HEAD, HEAD)],
                    out_ref.at[pl.ds((i * heads + head) * half, half), :],
                    sem.at[1 + i * heads + head],
                )
            )
    for copy in copies:
        copy.start()
    gates.wait()
    gate = gate_ref[...]
    high = gate.astype(jnp.bfloat16).astype(jnp.float32)
    parts = [high, gate - high]
    spare = gate_rows(heads) - 2 * heads
    if spare:
        parts.append(jnp.zeros((spare, length), jnp.float32))
    out_ref[2 * heads * half :, :] = jnp.concatenate(parts, axis=0).astype(jnp.bfloat16)
    for copy in copies:
        copy.wait()


def own_kernel(n_feat, *refs):
    sources, outs, bufs, sem = refs[:9], refs[9:15], refs[15:24], refs[24]
    qa_ref, acc_ref, own_ref, row_ref, fork_out, gate_out = outs
    q_ref, k_ref, v_ref, g_ref, cq_ref, ckv_ref, tok_ref, fork_ref, slot_ref = bufs

    ctx = lax.axis_index("ctx")
    feat = lax.axis_index("feat")
    rows = q_ref.shape[0]
    length, width = k_ref.shape
    heads = width // HEAD
    padded = qa_ref.shape[1] - GROUP * rows
    start = pl.multiple_of(feat * rows, rows)
    copies = []
    for i, (source, buf) in enumerate(zip(sources, bufs)):
        origin = source.at[pl.ds(start, rows), :] if i == 0 else source
        copies.append(pltpu.make_async_copy(origin, buf, sem.at[i]))
    for copy in copies:
        copy.start()
    for copy in copies:
        copy.wait()

    gate = g_ref[...]
    upto = exact_dot(gate, triangle(length, lambda r, c: r <= c), (1, 0))
    after = exact_dot(gate, triangle(length, lambda r, c: r > c), (1, 0))
    gate_out[...] = jnp.broadcast_to(upto[:, length - 1 :], (heads, length))
    row = lax.broadcasted_iota(jnp.int32, (rows, length), 0) + start
    col = lax.broadcasted_iota(jnp.int32, (rows, length), 1)
    causal = col <= row
    row_sum = exact_dot(causal.astype(jnp.float32), gate, (1, 1))
    row_ref[...] = row_sum

    owned = tok_ref.shape[1] // (lax.axis_size("ctx") * n_feat)
    line = lax.broadcasted_iota(jnp.int32, (padded, 1), 0)
    slot = (ctx * n_feat + feat) * owned + lax.rem(line, owned)
    mine = slot_ref[...] == slot
    pick_id = jnp.sum(jnp.where(mine, tok_ref[...].astype(jnp.float32), 0.0), axis=1, keepdims=True)
    fork = jnp.sum(jnp.where(mine, fork_ref[...].astype(jnp.float32), 0.0), axis=1, keepdims=True)
    fork_out[...] = jnp.broadcast_to(fork.astype(jnp.int32), fork_out.shape)
    cands = cq_ref.shape[0]
    pick = (
        lax.broadcasted_iota(jnp.int32, (padded, cands), 1).astype(jnp.float32) == pick_id
    ).astype(jnp.bfloat16)

    ones = jnp.ones((length, HEAD), jnp.bfloat16)
    for head in range(heads):
        lanes = slice(head * HEAD, (head + 1) * HEAD)
        picked = dot(pick, cq_ref[:, head * GROUP * HEAD : (head + 1) * GROUP * HEAD], (1, 0))
        branch_q = jnp.zeros((padded, HEAD), jnp.float32)
        for member in range(GROUP):
            chosen = (line >= member * owned) & (line < (member + 1) * owned)
            branch_q = jnp.where(chosen, picked[:, member * HEAD : (member + 1) * HEAD], branch_q)
        for member in range(GROUP):
            column = (head * GROUP + member) * HEAD
            qa_ref[head, member * rows : (member + 1) * rows, :] = q_ref[:, column : column + HEAD]
        qa_ref[head, GROUP * rows :, :] = branch_q.astype(jnp.bfloat16)

        reach = jnp.where(causal, row_sum[:, head : head + 1] - upto[head : head + 1, :], MASKED)
        decay = jnp.exp(reach) * SCALE
        branch_decay = jnp.exp(after[head : head + 1, :]) * SCALE
        raw = dot(qa_ref[head], k_ref[:, lanes], (1, 1))
        square = raw * raw
        weights = [
            (square[m * rows : (m + 1) * rows] * decay).astype(jnp.bfloat16) for m in range(GROUP)
        ]
        weights.append((square[GROUP * rows :] * branch_decay).astype(jnp.bfloat16))
        value = jnp.concatenate([v_ref[:, lanes], ones], axis=1)
        acc_ref[head] = dot(jnp.concatenate(weights, axis=0), value, (1, 0))

        new_k = dot(pick, ckv_ref[:, 0, lanes], (1, 0))
        new_v = dot(pick, ckv_ref[:, 1, lanes], (1, 0))
        inner = jnp.sum(branch_q * new_k, axis=1, keepdims=True)
        weight = inner * inner * SCALE
        own_ref[head, :, :HEAD] = weight * new_v
        own_ref[head, :, HEAD:] = jnp.broadcast_to(weight, (padded, HEAD))


def weigh(square, row_part, branch_part, rows):
    members = (square.shape[0] - branch_part.shape[0]) // rows
    parts = [square[m * rows : (m + 1) * rows] * row_part for m in range(members)]
    parts.append(square[members * rows :] * branch_part)
    return jnp.concatenate(parts, axis=0).astype(jnp.bfloat16)


def early_kernel(partners, late_partner, *refs):
    count = len(partners)
    qa_ref, acc_ref, own_ref, row_ref, fork_ref, gate_ref = refs[:6]
    near, far = refs[6 : 6 + count], refs[6 + count : 6 + 2 * count]
    (
        plain_ref, scaled_ref, late_row_ref, late_branch_ref, out_ref, value_ref, key_ref, stage_ref,
        sem,
    ) = refs[6 + 2 * count :]
    ctx = lax.axis_index("ctx")
    first_core = lax.axis_index("feat") == 0
    rows = row_ref.shape[0]
    heads, total_rows, _ = qa_ref.shape
    split = GROUP * rows
    padded = total_rows - split
    length = gate_ref.shape[1]
    half = length // 2
    blocks = [partner(ctx) for partner in partners]
    late = late_partner(ctx)
    fork = fork_ref[...]
    value_ref[:, :, HEAD:] = jnp.ones((heads, count * length, HEAD), jnp.bfloat16)
    gates = [received_gates(ref, heads, first_core) for ref in near]
    zero = jnp.zeros((padded, length), jnp.float32)
    for head in range(heads):
        for i in range(count):
            for j, ref in enumerate((near[i], far[i])):
                here = slice(i * length + j * half, i * length + (j + 1) * half)
                key_ref[head, here, :] = ref[head * half : (head + 1) * half, :]
                value_ref[head, here, :HEAD] = ref[
                    (heads + head) * half : (heads + head + 1) * half, :
                ]

    def body(first):
        raws = [dot(qa_ref[head, first:], key_ref[head], (1, 1)) for head in range(heads)]
        weights = []
        keeps = []
        for head in range(heads):
            at = slice(head, head + 1)
            row_h = row_ref[:, at]
            own_total = gate_ref[at, :]
            square = raws[head] * raws[head]
            kept = zero
            late_row = jnp.zeros((1, length), jnp.float32)
            late_branch = jnp.where((ctx > late) & (ctx < fork), own_total, zero)
            plains, scaleds = [], []
            for b, block in enumerate(blocks):
                after, total = gates[b][0][at, :], gates[b][1][at, :]
                kept = kept + jnp.where((block > ctx) & (block < fork), total, 0.0)
                late_row = late_row + jnp.where((block > late) & (block < ctx), total, 0.0)
                late_branch = late_branch + jnp.where((block > late) & (block < fork), total, 0.0)
                between = after
                past = after + jnp.where((ctx > block) & (ctx < fork), own_total, zero)
                for o, other in enumerate(blocks):
                    if o != b:
                        step = gates[o][1][at, :]
                        between = between + jnp.where((other > block) & (other < ctx), step, 0.0)
                        past = past + jnp.where((other > block) & (other < fork), step, 0.0)
                branch_decay = jnp.exp(jnp.where(block < fork, past, MASKED)) * SCALE
                crossed = (late > block) & (late < ctx)
                branch_crossed = (late > block) & (late < fork)
                decay = None
                if first == 0:
                    decay = jnp.exp(jnp.where(block < ctx, row_h + between, MASKED)) * SCALE
                part = square[:, b * length : (b + 1) * length]
                plains.append(
                    weigh(
                        part,
                        None if decay is None else jnp.where(crossed, 0.0, decay),
                        jnp.where(branch_crossed, 0.0, branch_decay),
                        rows,
                    )
                )
                scaleds.append(
                    weigh(
                        part,
                        None if decay is None else jnp.where(crossed, decay, 0.0),
                        jnp.where(branch_crossed, branch_decay, 0.0),
                        rows,
                    )
                )
            weights.append((jnp.concatenate(plains, axis=1), jnp.concatenate(scaleds, axis=1)))
            keeps.append(jnp.exp(jnp.where(ctx < fork, kept, MASKED)))
            late_row_ref[at, :] = jnp.where(late < ctx, late_row, MASKED)
            late_branch_ref[head] = jnp.where(late < fork, late_branch, MASKED)
        crossed = (late > ctx) & (late < fork)
        for head in range(heads):
            plain, scaled = [dot(w, value_ref[head], (1, 0)) for w in weights[head]]
            if first == 0:
                plain_ref[head, :split] = plain[:split] + acc_ref[head, :split, :]
                scaled_ref[head, :split] = scaled[:split]
            before = acc_ref[head, split:, :]
            for side in range(2):
                cols = slice(side * HEAD, (side + 1) * HEAD)
                moved = keeps[head] * before[:, cols]
                plain_ref[head, split:, cols] = (
                    plain[split - first :, cols]
                    + own_ref[head, :, cols]
                    + jnp.where(crossed, 0.0, moved)
                )
                scaled_ref[head, split:, cols] = scaled[split - first :, cols] + jnp.where(
                    crossed, moved, 0.0
                )

    needed = functools.reduce(jnp.logical_or, [block < ctx for block in blocks])
    pl.when(needed)(functools.partial(body, 0))
    pl.when(jnp.logical_not(needed))(functools.partial(body, split))

    def finish(ref):
        for head in range(heads):
            put_rows(head, ref[head, :split], stage_ref, out_ref, sem).start()
        for head in range(heads):
            rows_copy(head, stage_ref, out_ref, sem).wait()

    pl.when(needed & (late > ctx))(functools.partial(finish, plain_ref))
    pl.when(jnp.logical_not(needed) & (late > ctx))(functools.partial(finish, acc_ref))


def rows_copy(head, stage_ref, out_ref, sem):
    wide = pl.ds(head * GROUP * HEAD, GROUP * HEAD)
    return pltpu.make_async_copy(stage_ref.at[:, wide], out_ref.at[:, wide], sem.at[head])


def put_rows(head, total, stage_ref, out_ref, sem):
    rows = stage_ref.shape[0]
    ratio = total[:, :HEAD] / jnp.maximum(total[:, HEAD:], 1.0)
    for member in range(GROUP):
        column = (head * GROUP + member) * HEAD
        stage_ref[:, column : column + HEAD] = ratio[member * rows : (member + 1) * rows].astype(
            stage_ref.dtype
        )
    return rows_copy(head, stage_ref, out_ref, sem)


def half_products(qa_ref, ref, first, row_parts, branch_parts, rows):
    heads = qa_ref.shape[0]
    half = branch_parts[0].shape[1]
    raws = [
        dot(qa_ref[head, first:], ref[head * half : (head + 1) * half, :], (1, 1))
        for head in range(heads)
    ]
    weights = [
        weigh(raws[head] * raws[head], row_parts[head], branch_parts[head], rows)
        for head in range(heads)
    ]
    ones = jnp.ones((half, HEAD), jnp.bfloat16)
    sums = []
    for head in range(heads):
        value = ref[(heads + head) * half : (heads + head + 1) * half, :]
        sums.append(dot(weights[head], jnp.concatenate([value, ones], axis=1), (1, 0)))
    return sums


def near_kernel(
    late_partner,
    qa_ref, row_ref, plain_ref, scaled_ref, late_row_ref, late_branch_ref, near_ref,
    sum_ref, decay_ref, branch_decay_ref,
):
    heads = qa_ref.shape[0]
    rows = row_ref.shape[0]
    half = decay_ref.shape[2]
    ctx = lax.axis_index("ctx")
    first_core = lax.axis_index("feat") == 0
    after, total = received_gates(near_ref, heads, first_core)
    factor = jnp.exp(total)

    def body(first):
        decays, branch_decays = [], []
        for head in range(heads):
            at = slice(head, head + 1)
            if first == 0:
                decay = jnp.exp(row_ref[:, at] + (late_row_ref[at, :] + after[at, :])) * SCALE
                decay_ref[head] = decay[:, half:]
                decays.append(decay[:, :half])
            else:
                decays.append(None)
            branch_decay = jnp.exp(late_branch_ref[head] + after[at, :]) * SCALE
            branch_decay_ref[head] = branch_decay[:, half:]
            branch_decays.append(branch_decay[:, :half])
        sums = half_products(qa_ref, near_ref, first, decays, branch_decays, rows)
        for head in range(heads):
            for side in range(2):
                cols = slice(side * HEAD, (side + 1) * HEAD)
                sum_ref[head, first:, cols] = sums[head][:, cols] + (
                    plain_ref[head, first:, cols]
                    + factor[head : head + 1, :] * scaled_ref[head, first:, cols]
                )

    needed = late_partner(ctx) < ctx
    pl.when(needed)(functools.partial(body, 0))
    pl.when(jnp.logical_not(needed))(functools.partial(body, GROUP * rows))


def final_kernel(
    late_partner,
    qa_ref, sum_ref, decay_ref, branch_decay_ref, far_ref, done_ref,
    out_ref, branch_ref,
    stage_ref, branch_stage_ref, line_ref, sem,
):
    del done_ref
    heads = qa_ref.shape[0]
    rows = out_ref.shape[0]
    owned = branch_ref.shape[0]
    split = GROUP * rows
    ctx = lax.axis_index("ctx")

    def branches(head, total):
        line_ref[head] = total[:, :HEAD] / jnp.maximum(total[:, HEAD:], 1.0)
        for member in range(GROUP):
            column = (head * GROUP + member) * HEAD
            branch_stage_ref[:, column : column + HEAD] = line_ref[
                head, member * owned : (member + 1) * owned, :
            ].astype(branch_ref.dtype)

    last = pltpu.make_async_copy(branch_stage_ref, branch_ref, sem.at[heads])
    branch_parts = [branch_decay_ref[head] for head in range(heads)]

    def whole():
        row_parts = [decay_ref[head] for head in range(heads)]
        sums = half_products(qa_ref, far_ref, 0, row_parts, branch_parts, rows)
        for head in range(heads):
            total = sum_ref[head, :split] + sums[head][:split]
            put_rows(head, total, stage_ref, out_ref, sem).start()
            branches(head, sum_ref[head, split:] + sums[head][split:])
        last.start()
        for head in range(heads):
            rows_copy(head, stage_ref, out_ref, sem).wait()
        last.wait()

    def only_branches():
        sums = half_products(qa_ref, far_ref, split, [None] * heads, branch_parts, rows)
        for head in range(heads):
            branches(head, sum_ref[head, split:] + sums[head])
        last.start()
        last.wait()

    needed = late_partner(ctx) < ctx
    pl.when(needed)(whole)
    pl.when(jnp.logical_not(needed))(only_branches)


def swaps(count):
    if count & (count - 1) == 0:
        return [
            ([(i, i ^ step) for i in range(count)], functools.partial(lambda s, i: i ^ s, step))
            for step in range(1, count)
        ]
    return [
        (
            [(i, (i + step) % count) for i in range(count)],
            functools.partial(lambda s, i: lax.rem(i + count - s, count), step),
        )
        for step in range(1, count)
    ]


ORDER = (2, 1, 3)


def call(kernel, operands, outs, scratch=(), vmem=16 << 20, results=None, inputs=None,
         aliases=None):
    spec = pl.BlockSpec(memory_space=pltpu.VMEM)
    return pl.pallas_call(
        kernel,
        out_shape=outs,
        in_specs=inputs or [spec] * len(operands),
        out_specs=results or (spec,) * len(outs),
        scratch_shapes=list(scratch),
        compiler_params=pltpu.CompilerParams(vmem_limit_bytes=vmem),
        cost_estimate=pl.CostEstimate(flops=1 << 29, bytes_accessed=4 << 20, transcendentals=0),
        input_output_aliases=aliases or {},
    )(*operands)


def per_device(queries, keys, values, log_gate, cand_q, cand_kv, token_ids, fork_pos, slot_map):
    n_ctx = lax.axis_size("ctx")
    n_feat = lax.axis_size("feat")
    length, width = keys.shape
    heads = width // HEAD
    rows = length // n_feat
    half = length // 2
    branches = token_ids.shape[0]
    owned = branches // (n_ctx * n_feat)
    padded = -(-GROUP * owned // 16) * 16
    total_rows = GROUP * rows + padded
    assert n_feat == 2 and length == HEAD
    f32, bf16 = jnp.float32, jnp.bfloat16
    shape = jax.ShapeDtypeStruct

    hbm = pl.BlockSpec(memory_space=pltpu.HBM)
    in_hbm = lambda x: pltpu.with_memory_space_constraint(x, pltpu.HBM)
    gates = in_hbm(log_gate.T)
    (payload,) = call(
        pack_kernel, [in_hbm(keys), in_hbm(values), gates],
        (shape((2 * heads * half + gate_rows(heads), HEAD), bf16),),
        [pltpu.VMEM(gates.shape, f32), pltpu.SemaphoreType.DMA((1 + 2 * heads,))],
        vmem=4 << 20, inputs=[hbm] * 3,
    )
    pairings = swaps(n_ctx)
    count = len(pairings)
    steps = [s - 1 for s in ORDER] if count == 3 else list(range(count))
    near, far = [], []
    for s in steps:
        near.append(lax.ppermute(payload, "ctx", pairings[s][0]))
    for part in near:
        far.append(lax.ppermute(part, "feat", [(0, 1), (1, 0)]))
    partners = [pairings[s][1] for s in steps]

    sources = [
        queries, keys, values, gates, cand_q, cand_kv,
        token_ids[None], fork_pos[None], slot_map[None],
    ]
    wide = shape((heads, total_rows, 2 * HEAD), f32)
    queries_all, acc, token, row_sum, fork, total = call(
        functools.partial(own_kernel, n_feat), [in_hbm(s) for s in sources],
        (
            shape((heads, total_rows, HEAD), bf16),
            wide,
            shape((heads, padded, 2 * HEAD), f32),
            shape((rows, heads), f32),
            shape((padded, length), jnp.int32),
            shape((heads, length), f32),
        ),
        [pltpu.VMEM((rows, queries.shape[1]), queries.dtype)]
        + [pltpu.VMEM(s.shape, s.dtype) for s in sources[1:]]
        + [pltpu.SemaphoreType.DMA((len(sources),))],
        inputs=[hbm] * len(sources),
    )
    early = (count - 1) * length
    plain, scaled, late_row, late_branch, rows_out = call(
        functools.partial(early_kernel, partners[:-1], partners[-1]),
        [queries_all, acc, token, row_sum, fork, total, *near[:-1], *far[:-1]],
        (
            wide, wide, shape((heads, length), f32), shape((heads, padded, length), f32),
            shape((rows, queries.shape[1]), bf16),
        ),
        [
            pltpu.VMEM((heads, early, 2 * HEAD), bf16),
            pltpu.VMEM((heads, early, HEAD), bf16),
            pltpu.VMEM((rows, queries.shape[1]), bf16),
            pltpu.SemaphoreType.DMA((heads,)),
        ],
        results=(pl.BlockSpec(memory_space=pltpu.VMEM),) * 4 + (hbm,),
    )
    sums, decay, branch_decay = call(
        functools.partial(near_kernel, partners[-1]),
        [queries_all, row_sum, plain, scaled, late_row, late_branch, near[-1]],
        (wide, shape((heads, rows, half), f32), shape((heads, padded, half), f32)),
    )
    return call(
        functools.partial(final_kernel, partners[-1]),
        [queries_all, sums, decay, branch_decay, far[-1], in_hbm(rows_out)],
        (shape((rows, queries.shape[1]), bf16), shape((owned, queries.shape[1]), bf16)),
        [
            pltpu.VMEM((rows, queries.shape[1]), bf16),
            pltpu.VMEM((owned, queries.shape[1]), bf16),
            pltpu.VMEM((heads, padded, HEAD), f32),
            pltpu.SemaphoreType.DMA((heads + 1,)),
        ],
        results=(hbm, hbm), inputs=[pl.BlockSpec(memory_space=pltpu.VMEM)] * 5 + [hbm],
        aliases={5: 0},
    )


def solution(mesh):
    return sharded(mesh)


def sharded(mesh):
    return jax.shard_map(
        per_device,
        mesh=mesh,
        in_specs=(
            P(("groups", "ctx"), "head"),
            P(("groups", "ctx"), "head"),
            P(("groups", "ctx"), "head"),
            P(("groups", "ctx"), "head"),
            P("groups", "head"),
            P("groups", None, "head"),
            P("groups"),
            P("groups"),
            P("groups"),
        ),
        out_specs=(P(("groups", "ctx", "feat"), "head"), P(("groups", "ctx", "feat"), "head")),
        check_vma=False,
    )
```

```python
import functools

import jax
import jax.numpy as jnp
from jax import lax
from jax.experimental import pallas as pl
from jax.experimental.pallas import tpu as pltpu
from jax.sharding import PartitionSpec as P


HEAD = 128
GROUP = 5
MASKED = -1e30
SCALE = 1.0 / HEAD


def dot(a, b, contract, precision=None):
    return lax.dot_general(
        a, b, ((contract[:1], contract[1:]), ((), ())),
        precision=precision, preferred_element_type=jnp.float32,
    )


def exact_dot(a, b, contract):
    return dot(a, b, contract, lax.Precision.HIGHEST)


def triangle(length, keep):
    row = lax.broadcasted_iota(jnp.int32, (length, length), 0)
    col = lax.broadcasted_iota(jnp.int32, (length, length), 1)
    return keep(row, col).astype(jnp.float32)


def received_gates(ref, heads, first_core):
    tile = ref[ref.shape[0] - gate_rows(heads) :, :].astype(jnp.float32)
    gate = tile + pltpu.roll(tile, tile.shape[0] - heads, 0)
    length = gate.shape[1]
    after = exact_dot(gate, triangle(length, lambda r, c: r > c), (1, 0))
    total = exact_dot(gate, triangle(length, lambda r, c: r >= 0), (1, 0))
    after = jnp.where(first_core, after, pltpu.roll(after, length // 2, 1))
    return after, total


def gate_rows(heads):
    return -(-2 * heads // 8) * 8


def pack_kernel(k_ref, v_ref, g_ref, out_ref, gate_ref, sem):
    length, width = k_ref.shape
    heads = width // HEAD
    half = length // 2
    start = pl.multiple_of(lax.axis_index("feat") * half, half)
    gates = pltpu.make_async_copy(g_ref, gate_ref, sem.at[0])
    gates.start()
    copies = []
    for i, ref in enumerate((k_ref, v_ref)):
        for head in range(heads):
            copies.append(
                pltpu.make_async_copy(
                    ref.at[pl.ds(start, half), pl.ds(head * HEAD, HEAD)],
                    out_ref.at[pl.ds((i * heads + head) * half, half), :],
                    sem.at[1 + i * heads + head],
                )
            )
    for copy in copies:
        copy.start()
    gates.wait()
    gate = gate_ref[...]
    high = gate.astype(jnp.bfloat16).astype(jnp.float32)
    parts = [high, gate - high]
    spare = gate_rows(heads) - 2 * heads
    if spare:
        parts.append(jnp.zeros((spare, length), jnp.float32))
    out_ref[2 * heads * half :, :] = jnp.concatenate(parts, axis=0).astype(jnp.bfloat16)
    for copy in copies:
        copy.wait()


def own_kernel(n_feat, partners, *refs):
    sources, outs, bufs = refs[:9], refs[9:15], refs[16:25]
    out_ref, sem, stage_ref, row_sem = refs[15], *refs[25:]
    qa_ref, acc_ref, own_ref, row_ref, fork_out, gate_out = outs
    q_ref, k_ref, v_ref, g_ref, cq_ref, ckv_ref, tok_ref, fork_ref, slot_ref = bufs

    ctx = lax.axis_index("ctx")
    feat = lax.axis_index("feat")
    rows = q_ref.shape[0]
    length, width = k_ref.shape
    heads = width // HEAD
    padded = qa_ref.shape[1] - GROUP * rows
    start = pl.multiple_of(feat * rows, rows)
    copies = []
    for i, (source, buf) in enumerate(zip(sources, bufs)):
        origin = source.at[pl.ds(start, rows), :] if i == 0 else source
        copies.append(pltpu.make_async_copy(origin, buf, sem.at[i]))
    for copy in copies:
        copy.start()
    for copy in copies:
        copy.wait()

    gate = g_ref[...]
    upto = exact_dot(gate, triangle(length, lambda r, c: r <= c), (1, 0))
    after = exact_dot(gate, triangle(length, lambda r, c: r > c), (1, 0))
    gate_out[...] = jnp.broadcast_to(upto[:, length - 1 :], (heads, length))
    row = lax.broadcasted_iota(jnp.int32, (rows, length), 0) + start
    col = lax.broadcasted_iota(jnp.int32, (rows, length), 1)
    causal = col <= row
    row_sum = exact_dot(causal.astype(jnp.float32), gate, (1, 1))
    row_ref[...] = row_sum

    owned = tok_ref.shape[1] // (lax.axis_size("ctx") * n_feat)
    line = lax.broadcasted_iota(jnp.int32, (padded, 1), 0)
    slot = (ctx * n_feat + feat) * owned + lax.rem(line, owned)
    mine = slot_ref[...] == slot
    pick_id = jnp.sum(jnp.where(mine, tok_ref[...].astype(jnp.float32), 0.0), axis=1, keepdims=True)
    fork = jnp.sum(jnp.where(mine, fork_ref[...].astype(jnp.float32), 0.0), axis=1, keepdims=True)
    fork_out[...] = jnp.broadcast_to(fork.astype(jnp.int32), fork_out.shape)
    cands = cq_ref.shape[0]
    pick = (
        lax.broadcasted_iota(jnp.int32, (padded, cands), 1).astype(jnp.float32) == pick_id
    ).astype(jnp.bfloat16)

    ones = jnp.ones((length, HEAD), jnp.bfloat16)
    for head in range(heads):
        lanes = slice(head * HEAD, (head + 1) * HEAD)
        picked = dot(pick, cq_ref[:, head * GROUP * HEAD : (head + 1) * GROUP * HEAD], (1, 0))
        branch_q = jnp.zeros((padded, HEAD), jnp.float32)
        for member in range(GROUP):
            chosen = (line >= member * owned) & (line < (member + 1) * owned)
            branch_q = jnp.where(chosen, picked[:, member * HEAD : (member + 1) * HEAD], branch_q)
        for member in range(GROUP):
            column = (head * GROUP + member) * HEAD
            qa_ref[head, member * rows : (member + 1) * rows, :] = q_ref[:, column : column + HEAD]
        qa_ref[head, GROUP * rows :, :] = branch_q.astype(jnp.bfloat16)

        reach = jnp.where(causal, row_sum[:, head : head + 1] - upto[head : head + 1, :], MASKED)
        decay = jnp.exp(reach) * SCALE
        branch_decay = jnp.exp(after[head : head + 1, :]) * SCALE
        raw = dot(qa_ref[head], k_ref[:, lanes], (1, 1))
        square = raw * raw
        weights = [
            (square[m * rows : (m + 1) * rows] * decay).astype(jnp.bfloat16) for m in range(GROUP)
        ]
        weights.append((square[GROUP * rows :] * branch_decay).astype(jnp.bfloat16))
        value = jnp.concatenate([v_ref[:, lanes], ones], axis=1)
        acc_ref[head] = dot(jnp.concatenate(weights, axis=0), value, (1, 0))

        new_k = dot(pick, ckv_ref[:, 0, lanes], (1, 0))
        new_v = dot(pick, ckv_ref[:, 1, lanes], (1, 0))
        inner = jnp.sum(branch_q * new_k, axis=1, keepdims=True)
        weight = inner * inner * SCALE
        own_ref[head, :, :HEAD] = weight * new_v
        own_ref[head, :, HEAD:] = jnp.broadcast_to(weight, (padded, HEAD))

    @pl.when(functools.reduce(jnp.logical_and, [partner(ctx) > ctx for partner in partners]))
    def _():
        for head in range(heads):
            put_rows(head, acc_ref[head, : GROUP * rows], stage_ref, out_ref, row_sem).start()
        for head in range(heads):
            rows_copy(head, stage_ref, out_ref, row_sem).wait()


def weigh(square, row_part, branch_part, rows):
    members = (square.shape[0] - branch_part.shape[0]) // rows
    parts = [square[m * rows : (m + 1) * rows] * row_part for m in range(members)]
    parts.append(square[members * rows :] * branch_part)
    return jnp.concatenate(parts, axis=0).astype(jnp.bfloat16)


def early_kernel(partners, late_partner, *refs):
    count = len(partners)
    qa_ref, acc_ref, own_ref, row_ref, fork_ref, gate_ref = refs[:6]
    near, far = refs[6 : 6 + count], refs[6 + count : 6 + 2 * count]
    (
        plain_ref, scaled_ref, late_row_ref, late_branch_ref, out_ref, value_ref, key_ref, stage_ref,
        sem,
    ) = refs[7 + 2 * count :]
    ctx = lax.axis_index("ctx")
    first_core = lax.axis_index("feat") == 0
    rows = row_ref.shape[0]
    heads, total_rows, _ = qa_ref.shape
    split = GROUP * rows
    padded = total_rows - split
    length = gate_ref.shape[1]
    half = length // 2
    blocks = [partner(ctx) for partner in partners]
    late = late_partner(ctx)
    fork = fork_ref[...]
    value_ref[:, :, HEAD:] = jnp.ones((heads, count * length, HEAD), jnp.bfloat16)
    gates = [received_gates(ref, heads, first_core) for ref in near]
    zero = jnp.zeros((padded, length), jnp.float32)
    for head in range(heads):
        for i in range(count):
            for j, ref in enumerate((near[i], far[i])):
                here = slice(i * length + j * half, i * length + (j + 1) * half)
                key_ref[head, here, :] = ref[head * half : (head + 1) * half, :]
                value_ref[head, here, :HEAD] = ref[
                    (heads + head) * half : (heads + head + 1) * half, :
                ]

    def body(first):
        raws = [dot(qa_ref[head, first:], key_ref[head], (1, 1)) for head in range(heads)]
        weights = []
        keeps = []
        for head in range(heads):
            at = slice(head, head + 1)
            row_h = row_ref[:, at]
            own_total = gate_ref[at, :]
            square = raws[head] * raws[head]
            kept = zero
            late_row = jnp.zeros((1, length), jnp.float32)
            late_branch = jnp.where((ctx > late) & (ctx < fork), own_total, zero)
            plains, scaleds = [], []
            for b, block in enumerate(blocks):
                after, total = gates[b][0][at, :], gates[b][1][at, :]
                kept = kept + jnp.where((block > ctx) & (block < fork), total, 0.0)
                late_row = late_row + jnp.where((block > late) & (block < ctx), total, 0.0)
                late_branch = late_branch + jnp.where((block > late) & (block < fork), total, 0.0)
                between = after
                past = after + jnp.where((ctx > block) & (ctx < fork), own_total, zero)
                for o, other in enumerate(blocks):
                    if o != b:
                        step = gates[o][1][at, :]
                        between = between + jnp.where((other > block) & (other < ctx), step, 0.0)
                        past = past + jnp.where((other > block) & (other < fork), step, 0.0)
                branch_decay = jnp.exp(jnp.where(block < fork, past, MASKED)) * SCALE
                crossed = (late > block) & (late < ctx)
                branch_crossed = (late > block) & (late < fork)
                decay = None
                if first == 0:
                    decay = jnp.exp(jnp.where(block < ctx, row_h + between, MASKED)) * SCALE
                part = square[:, b * length : (b + 1) * length]
                plains.append(
                    weigh(
                        part,
                        None if decay is None else jnp.where(crossed, 0.0, decay),
                        jnp.where(branch_crossed, 0.0, branch_decay),
                        rows,
                    )
                )
                scaleds.append(
                    weigh(
                        part,
                        None if decay is None else jnp.where(crossed, decay, 0.0),
                        jnp.where(branch_crossed, branch_decay, 0.0),
                        rows,
                    )
                )
            weights.append((jnp.concatenate(plains, axis=1), jnp.concatenate(scaleds, axis=1)))
            keeps.append(jnp.exp(jnp.where(ctx < fork, kept, MASKED)))
            late_row_ref[at, :] = jnp.where(late < ctx, late_row, MASKED)
            late_branch_ref[head] = jnp.where(late < fork, late_branch, MASKED)
        crossed = (late > ctx) & (late < fork)
        for head in range(heads):
            plain, scaled = [dot(w, value_ref[head], (1, 0)) for w in weights[head]]
            if first == 0:
                plain_ref[head, :split] = plain[:split] + acc_ref[head, :split, :]
                scaled_ref[head, :split] = scaled[:split]
            before = acc_ref[head, split:, :]
            for side in range(2):
                cols = slice(side * HEAD, (side + 1) * HEAD)
                moved = keeps[head] * before[:, cols]
                plain_ref[head, split:, cols] = (
                    plain[split - first :, cols]
                    + own_ref[head, :, cols]
                    + jnp.where(crossed, 0.0, moved)
                )
                scaled_ref[head, split:, cols] = scaled[split - first :, cols] + jnp.where(
                    crossed, moved, 0.0
                )

    needed = functools.reduce(jnp.logical_or, [block < ctx for block in blocks])
    pl.when(needed)(functools.partial(body, 0))
    pl.when(jnp.logical_not(needed))(functools.partial(body, split))

    @pl.when(needed & (late > ctx))
    def _():
        for head in range(heads):
            put_rows(head, plain_ref[head, :split], stage_ref, out_ref, sem).start()
        for head in range(heads):
            rows_copy(head, stage_ref, out_ref, sem).wait()


def rows_copy(head, stage_ref, out_ref, sem):
    wide = pl.ds(head * GROUP * HEAD, GROUP * HEAD)
    return pltpu.make_async_copy(stage_ref.at[:, wide], out_ref.at[:, wide], sem.at[head])


def put_rows(head, total, stage_ref, out_ref, sem):
    rows = stage_ref.shape[0]
    ratio = total[:, :HEAD] / jnp.maximum(total[:, HEAD:], 1.0)
    for member in range(GROUP):
        column = (head * GROUP + member) * HEAD
        stage_ref[:, column : column + HEAD] = ratio[member * rows : (member + 1) * rows].astype(
            stage_ref.dtype
        )
    return rows_copy(head, stage_ref, out_ref, sem)


def half_products(qa_ref, ref, first, row_parts, branch_parts, rows):
    heads = qa_ref.shape[0]
    half = branch_parts[0].shape[1]
    raws = [
        dot(qa_ref[head, first:], ref[head * half : (head + 1) * half, :], (1, 1))
        for head in range(heads)
    ]
    weights = [
        weigh(raws[head] * raws[head], row_parts[head], branch_parts[head], rows)
        for head in range(heads)
    ]
    ones = jnp.ones((half, HEAD), jnp.bfloat16)
    sums = []
    for head in range(heads):
        value = ref[(heads + head) * half : (heads + head + 1) * half, :]
        sums.append(dot(weights[head], jnp.concatenate([value, ones], axis=1), (1, 0)))
    return sums


def near_kernel(
    late_partner,
    qa_ref, row_ref, plain_ref, scaled_ref, late_row_ref, late_branch_ref, near_ref,
    sum_ref, decay_ref, branch_decay_ref,
):
    heads = qa_ref.shape[0]
    rows = row_ref.shape[0]
    half = decay_ref.shape[2]
    ctx = lax.axis_index("ctx")
    first_core = lax.axis_index("feat") == 0
    after, total = received_gates(near_ref, heads, first_core)
    factor = jnp.exp(total)

    def body(first):
        decays, branch_decays = [], []
        for head in range(heads):
            at = slice(head, head + 1)
            if first == 0:
                decay = jnp.exp(row_ref[:, at] + (late_row_ref[at, :] + after[at, :])) * SCALE
                decay_ref[head] = decay[:, half:]
                decays.append(decay[:, :half])
            else:
                decays.append(None)
            branch_decay = jnp.exp(late_branch_ref[head] + after[at, :]) * SCALE
            branch_decay_ref[head] = branch_decay[:, half:]
            branch_decays.append(branch_decay[:, :half])
        sums = half_products(qa_ref, near_ref, first, decays, branch_decays, rows)
        for head in range(heads):
            for side in range(2):
                cols = slice(side * HEAD, (side + 1) * HEAD)
                sum_ref[head, first:, cols] = sums[head][:, cols] + (
                    plain_ref[head, first:, cols]
                    + factor[head : head + 1, :] * scaled_ref[head, first:, cols]
                )

    needed = late_partner(ctx) < ctx
    pl.when(needed)(functools.partial(body, 0))
    pl.when(jnp.logical_not(needed))(functools.partial(body, GROUP * rows))


def final_kernel(
    late_partner,
    qa_ref, sum_ref, decay_ref, branch_decay_ref, far_ref, done_ref,
    out_ref, branch_ref,
    stage_ref, branch_stage_ref, line_ref, sem,
):
    del done_ref
    heads = qa_ref.shape[0]
    rows = out_ref.shape[0]
    owned = branch_ref.shape[0]
    split = GROUP * rows
    ctx = lax.axis_index("ctx")

    def branches(head, total):
        line_ref[head] = total[:, :HEAD] / jnp.maximum(total[:, HEAD:], 1.0)
        for member in range(GROUP):
            column = (head * GROUP + member) * HEAD
            branch_stage_ref[:, column : column + HEAD] = line_ref[
                head, member * owned : (member + 1) * owned, :
            ].astype(branch_ref.dtype)

    last = pltpu.make_async_copy(branch_stage_ref, branch_ref, sem.at[heads])
    branch_parts = [branch_decay_ref[head] for head in range(heads)]

    def whole():
        row_parts = [decay_ref[head] for head in range(heads)]
        sums = half_products(qa_ref, far_ref, 0, row_parts, branch_parts, rows)
        for head in range(heads):
            total = sum_ref[head, :split] + sums[head][:split]
            put_rows(head, total, stage_ref, out_ref, sem).start()
            branches(head, sum_ref[head, split:] + sums[head][split:])
        last.start()
        for head in range(heads):
            rows_copy(head, stage_ref, out_ref, sem).wait()
        last.wait()

    def only_branches():
        sums = half_products(qa_ref, far_ref, split, [None] * heads, branch_parts, rows)
        for head in range(heads):
            branches(head, sum_ref[head, split:] + sums[head])
        last.start()
        last.wait()

    needed = late_partner(ctx) < ctx
    pl.when(needed)(whole)
    pl.when(jnp.logical_not(needed))(only_branches)


def swaps(count):
    if count & (count - 1) == 0:
        return [
            ([(i, i ^ step) for i in range(count)], functools.partial(lambda s, i: i ^ s, step))
            for step in range(1, count)
        ]
    return [
        (
            [(i, (i + step) % count) for i in range(count)],
            functools.partial(lambda s, i: lax.rem(i + count - s, count), step),
        )
        for step in range(1, count)
    ]


ORDER = (2, 1, 3)


def call(kernel, operands, outs, scratch=(), vmem=16 << 20, results=None, inputs=None,
         aliases=None):
    spec = pl.BlockSpec(memory_space=pltpu.VMEM)
    return pl.pallas_call(
        kernel,
        out_shape=outs,
        in_specs=inputs or [spec] * len(operands),
        out_specs=results or (spec,) * len(outs),
        scratch_shapes=list(scratch),
        compiler_params=pltpu.CompilerParams(vmem_limit_bytes=vmem),
        cost_estimate=pl.CostEstimate(flops=1 << 29, bytes_accessed=4 << 20, transcendentals=0),
        input_output_aliases=aliases or {},
    )(*operands)


def per_device(queries, keys, values, log_gate, cand_q, cand_kv, token_ids, fork_pos, slot_map):
    n_ctx = lax.axis_size("ctx")
    n_feat = lax.axis_size("feat")
    length, width = keys.shape
    heads = width // HEAD
    rows = length // n_feat
    half = length // 2
    branches = token_ids.shape[0]
    owned = branches // (n_ctx * n_feat)
    padded = -(-GROUP * owned // 16) * 16
    total_rows = GROUP * rows + padded
    assert n_feat == 2 and length == HEAD
    f32, bf16 = jnp.float32, jnp.bfloat16
    shape = jax.ShapeDtypeStruct

    hbm = pl.BlockSpec(memory_space=pltpu.HBM)
    in_hbm = lambda x: pltpu.with_memory_space_constraint(x, pltpu.HBM)
    gates = in_hbm(log_gate.T)
    (payload,) = call(
        pack_kernel, [in_hbm(keys), in_hbm(values), gates],
        (shape((2 * heads * half + gate_rows(heads), HEAD), bf16),),
        [pltpu.VMEM(gates.shape, f32), pltpu.SemaphoreType.DMA((1 + 2 * heads,))],
        vmem=4 << 20, inputs=[hbm] * 3,
    )
    pairings = swaps(n_ctx)
    count = len(pairings)
    steps = [s - 1 for s in ORDER] if count == 3 else list(range(count))
    near, far = [], []
    for s in steps:
        near.append(lax.ppermute(payload, "ctx", pairings[s][0]))
    for part in near:
        far.append(lax.ppermute(part, "feat", [(0, 1), (1, 0)]))
    partners = [pairings[s][1] for s in steps]

    sources = [
        queries, keys, values, gates, cand_q, cand_kv,
        token_ids[None], fork_pos[None], slot_map[None],
    ]
    wide = shape((heads, total_rows, 2 * HEAD), f32)
    vmem = pl.BlockSpec(memory_space=pltpu.VMEM)
    rows_shape = shape((rows, queries.shape[1]), bf16)
    queries_all, acc, token, row_sum, fork, total, rows_out = call(
        functools.partial(own_kernel, n_feat, partners), [in_hbm(s) for s in sources],
        (
            shape((heads, total_rows, HEAD), bf16),
            wide,
            shape((heads, padded, 2 * HEAD), f32),
            shape((rows, heads), f32),
            shape((padded, length), jnp.int32),
            shape((heads, length), f32),
            rows_shape,
        ),
        [pltpu.VMEM((rows, queries.shape[1]), queries.dtype)]
        + [pltpu.VMEM(s.shape, s.dtype) for s in sources[1:]]
        + [pltpu.SemaphoreType.DMA((len(sources),))]
        + [pltpu.VMEM(rows_shape.shape, bf16), pltpu.SemaphoreType.DMA((heads,))],
        inputs=[hbm] * len(sources), results=(vmem,) * 6 + (hbm,),
    )
    early = (count - 1) * length
    plain, scaled, late_row, late_branch, rows_out = call(
        functools.partial(early_kernel, partners[:-1], partners[-1]),
        [queries_all, acc, token, row_sum, fork, total, *near[:-1], *far[:-1], in_hbm(rows_out)],
        (
            wide, wide, shape((heads, length), f32), shape((heads, padded, length), f32),
            rows_shape,
        ),
        [
            pltpu.VMEM((heads, early, 2 * HEAD), bf16),
            pltpu.VMEM((heads, early, HEAD), bf16),
            pltpu.VMEM((rows, queries.shape[1]), bf16),
            pltpu.SemaphoreType.DMA((heads,)),
        ],
        results=(vmem,) * 4 + (hbm,), inputs=[vmem] * (4 + 2 * count) + [hbm],
        aliases={4 + 2 * count: 4},
    )
    sums, decay, branch_decay = call(
        functools.partial(near_kernel, partners[-1]),
        [queries_all, row_sum, plain, scaled, late_row, late_branch, near[-1]],
        (wide, shape((heads, rows, half), f32), shape((heads, padded, half), f32)),
    )
    return call(
        functools.partial(final_kernel, partners[-1]),
        [queries_all, sums, decay, branch_decay, far[-1], in_hbm(rows_out)],
        (shape((rows, queries.shape[1]), bf16), shape((owned, queries.shape[1]), bf16)),
        [
            pltpu.VMEM((rows, queries.shape[1]), bf16),
            pltpu.VMEM((owned, queries.shape[1]), bf16),
            pltpu.VMEM((heads, padded, HEAD), f32),
            pltpu.SemaphoreType.DMA((heads + 1,)),
        ],
        results=(hbm, hbm), inputs=[vmem] * 5 + [hbm],
        aliases={5: 0},
    )


def solution(mesh):
    return sharded(mesh)


def sharded(mesh):
    return jax.shard_map(
        per_device,
        mesh=mesh,
        in_specs=(
            P(("groups", "ctx"), "head"),
            P(("groups", "ctx"), "head"),
            P(("groups", "ctx"), "head"),
            P(("groups", "ctx"), "head"),
            P("groups", "head"),
            P("groups", None, "head"),
            P("groups"),
            P("groups"),
            P("groups"),
        ),
        out_specs=(P(("groups", "ctx", "feat"), "head"), P(("groups", "ctx", "feat"), "head")),
        check_vma=False,
    )
```
